128 devices in a mesh: section: 8 (over y_hi, x), dom: 16 (over y_lo, z, core).
Axes of the slice: x: 4, y: 4 (y_hi: 2, y_lo: 2; y = y_hi * 2 + y_lo), z: 4, core: 2. Of those that a mesh axis runs over, the one named last changes fastest.
Arguments:
- features: bfloat16 [65536, 256], P(('section', 'dom')), may hold values from -6 to 6
- order: int32 [128, 512], P(('section', 'dom')), may hold values from 0 to 511, each once within a row
- tile_rows: int32 [8, 16, 192], P('section', 'dom'), may hold values from 0 to 63
- tile_cols: int32 [8, 16, 192], P('section', 'dom'), may hold values from 0 to 3
- tile_live: int32 [8, 16, 192], P('section', 'dom'), may hold values 0 or 1
- tile_values: bfloat16 [8, 16, 192, 128, 128], P('section', 'dom'), may hold values from -0.087890625 to 0.087890625
- weight: bfloat16 [256, 256], replicated, may hold values from -0.375 to 0.375
- cotangent: bfloat16 [65536, 256], P(('section', 'dom')), may hold values from -6 to 6
Outputs:
- activated: bfloat16 [65536, 256], P(('section', 'dom'))
- feature_grad: bfloat16 [65536, 256], P(('section', 'dom'))
- weight_grad: float32 [256, 256], replicated
The draws below stay inside these ranges and needn't reach their ends.
Inputs may be any that keep to these rules, and one draw needn't show every extreme that they name: `tile_cols`: tiles t of a device with t // 24 = j have their columns in section block j.
All inputs are finite; a program needn't handle non-finite values. No bound on the sum of `tile_live` on one device may be relied on, other than what follows from the above.
Results may differ from the reference program's by a relative error of at most 0.0063.
Values may be sent and summed in bfloat16 or wider, within the bound.
No kernel may reach another device: no remote copies, remote signals or barrier semaphores. Data moves between devices by JAX's collectives and lax.ppermute only.
A program may use at most 64 MiB of HBM per device.

```python
import jax
import jax.numpy as jnp
from jax import lax

F = 256
TILE = 128
BLK_DEV = 512
TPB = 24
TILES_DEV = 192
NODES = 65536
N_SECTION = 8
N_DOM = 16


def set_ends(drawn, rng, least, largest):
    dims = drawn.shape
    spot = [jax.random.randint(jax.random.fold_in(rng, axis), (), 0, dims[axis]) for axis in range(len(dims))]
    drawn = drawn.at[tuple(spot)].set(least)
    longest = dims.index(max(dims))
    spot[longest] = (spot[longest] + 1) % dims[longest]
    return drawn.at[tuple(spot)].set(largest)


def block_levels(key, dims, shards, smallest, largest):
    level = 1.0
    for axis_at, shards_of in shards:
        steps = jax.random.uniform(jax.random.fold_in(jax.random.fold_in(key, 6), axis_at), (shards_of,), jnp.float32, smallest / len(shards), largest / len(shards))
        level = level * jnp.repeat(jnp.exp(steps), dims[axis_at] // shards_of).reshape((-1,) + (1,) * (len(dims) - 1 - axis_at))
    return level


def noise(rng, shape, scale, reach, shards=(), held_as=jnp.bfloat16):
    level = block_levels(rng, shape, shards, -0.22, 0.18) if shards else 1.0
    drawn = jax.random.normal(rng, shape, jnp.float32) * scale * level
    return jnp.minimum(jnp.maximum(drawn, -reach), reach).astype(held_as)


def setup_inputs(seed: int = 0) -> dict:
    arg_keys = jax.random.split(jax.random.key(seed), 9)
    return {
        "features": noise(arg_keys[0], (NODES, F), 1.0, 6.0, ((0, 128),)),
        "order": jax.vmap(lambda own: jax.random.permutation(own, BLK_DEV))(jax.random.split(arg_keys[1], (N_SECTION * N_DOM))).reshape((N_SECTION * N_DOM, BLK_DEV)).astype(jnp.int32),
        "tile_rows": set_ends(jax.random.randint(arg_keys[2], (N_SECTION, N_DOM, TILES_DEV), 0, N_DOM * BLK_DEV // TILE), jax.random.fold_in(arg_keys[2], 1), 0, (N_DOM * BLK_DEV // TILE) - 1).astype(jnp.int32),
        "tile_cols": set_ends(jax.random.randint(arg_keys[3], (N_SECTION, N_DOM, TILES_DEV), 0, BLK_DEV // TILE), jax.random.fold_in(arg_keys[3], 1), 0, (BLK_DEV // TILE) - 1).astype(jnp.int32),
        "tile_live": set_ends((jax.random.randint(arg_keys[4], (N_SECTION, N_DOM, TILES_DEV), 0, 4) < 3).astype(jnp.int32), jax.random.fold_in(arg_keys[4], 1), 0, 1),
        "tile_values": noise(arg_keys[5], (N_SECTION, N_DOM, TILES_DEV, TILE, TILE), (1.15 * (TPB * N_SECTION * TILE * TILE // BLK_DEV) ** -0.5), 0.087890625, ((0, 8), (1, 16))),
        "weight": noise(arg_keys[6], (F, F), F ** -0.5, 0.375),
        "cotangent": noise(arg_keys[7], (NODES, F), 1.0, 6.0, ((0, 128),)),
    }


def reference(features, order, tile_rows, tile_cols, tile_live, tile_values, weight, cotangent):
    nblocks = N_SECTION * N_DOM
    column_block_index = BLK_DEV // TILE
    rowtiles = N_DOM * column_block_index
    ntiles = TPB * N_SECTION
    blocks = features.reshape(nblocks, BLK_DEV, F)
    reordered = jnp.take_along_axis(blocks, order[:, :, None], axis=1)
    tiled = reordered.reshape(nblocks * column_block_index, TILE, F)
    rows_all = tile_rows.reshape(nblocks, ntiles)
    cols_all = tile_cols.reshape(nblocks, ntiles)
    live_all = tile_live.reshape(nblocks, ntiles).astype(jnp.float32)
    vals_all = tile_values.reshape(nblocks, ntiles, TILE, TILE)
    group = (jnp.arange(ntiles) // TPB).astype(jnp.int32)

    def forward(acc, k):
        group_id = k // N_DOM
        member_id = k % N_DOM
        src = (group * N_DOM + member_id) * column_block_index + cols_all[k]
        piece = tiled[src].astype(jnp.float32)
        tile_product = jnp.einsum('dzm,dmx->dzx', vals_all[k].astype(jnp.float32), piece)
        tile_product = tile_product * live_all[k][:, None, None]
        return (acc.at[group_id * rowtiles + rows_all[k]].add(tile_product), None)
    acc = jnp.zeros((nblocks * column_block_index, TILE, F), jnp.float32)
    acc, _ = lax.scan(forward, acc, jnp.arange(nblocks, dtype=jnp.int32))
    agg_low = acc.reshape(NODES, F).astype(jnp.bfloat16)
    pre = jnp.dot(agg_low, weight, preferred_element_type=jnp.float32)
    activated = jax.nn.gelu(pre, approximate=True).astype(jnp.bfloat16)
    _, pull = jax.vjp(lambda v: jax.nn.gelu(v, approximate=True), pre)
    pre_grad = pull(cotangent.astype(jnp.float32))[0].astype(jnp.bfloat16)
    weight_grad = jnp.dot(agg_low.T, pre_grad, preferred_element_type=jnp.float32)
    agg_grad = jnp.dot(pre_grad, weight.T, preferred_element_type=jnp.float32).astype(jnp.bfloat16)
    grad_tiles = agg_grad.reshape(nblocks * column_block_index, TILE, F)

    def backward(acc2, k):
        group_id = k // N_DOM
        member_id = k % N_DOM
        piece = grad_tiles[group_id * rowtiles + rows_all[k]].astype(jnp.float32)
        tile_product = jnp.einsum('byw,bys->bws', vals_all[k].astype(jnp.float32), piece)
        tile_product = tile_product * live_all[k][:, None, None]
        dst = (group * N_DOM + member_id) * column_block_index + cols_all[k]
        return (acc2.at[dst].add(tile_product), None)
    acc2 = jnp.zeros((nblocks * column_block_index, TILE, F), jnp.float32)
    acc2, _ = lax.scan(backward, acc2, jnp.arange(nblocks, dtype=jnp.int32))
    grad_blocks = acc2.reshape(nblocks, BLK_DEV, F)
    placed = jax.vmap(lambda o, v: jnp.zeros_like(v).at[o].set(v))(order, grad_blocks)
    feature_grad = placed.reshape(NODES, F).astype(jnp.bfloat16)
    return (activated, feature_grad, weight_grad)
```

```python
import jax
import jax.numpy as jnp
from jax import lax
from jax.experimental import pallas as pl
from jax.experimental.pallas import tpu as pltpu
from jax.sharding import PartitionSpec as P

F32 = jnp.float32
BF16 = jnp.bfloat16
N = 8


def target(i, k):
    return ((i >> 2) ^ (k >> 2)) * 4 + ((i + k) & 3)


def source(i, k):
    return ((i >> 2) ^ (k >> 2)) * 4 + ((i - k) & 3)


def offset(i, j):
    return ((i >> 2) ^ (j >> 2)) * 4 + ((i - j) & 3)


def to_section(x, k):
    return lax.ppermute(x, "section", [(i, target(i, k)) for i in range(N)])


def to_chip(x, k):
    return lax.ppermute(x, "dom", [(2 * i + q, 2 * target(i, k) + q) for i in range(N) for q in range(2)])


def to_core(x):
    return lax.ppermute(x, "dom", [(d, d ^ 1) for d in range(2 * N)])


def forward_kernel(here, rows, cols, values, *refs):
    blocks, outs = refs[:N], refs[N : N + N + 1]
    theirs, mine = outs[0], outs[1:]
    vals, xs, acc, vsem, xsem = refs[N + N + 1 :]
    s, c, core = here[0], here[1], here[2]
    per = values.shape[0] // N
    tile = values.shape[1]
    pieces = xs.shape[1] // tile
    for k in range(N):
        j = source(s, k)
        pltpu.make_async_copy(blocks[k], xs.at[k], xsem.at[k]).start()
        pltpu.make_async_copy(values.at[pl.ds(j * per, per)], vals.at[k], vsem.at[k]).start()
    acc[...] = jnp.zeros_like(acc)
    for k in range(N):
        j = source(s, k)
        pltpu.make_async_copy(blocks[k], xs.at[k], xsem.at[k]).wait()
        pltpu.make_async_copy(values.at[pl.ds(j * per, per)], vals.at[k], vsem.at[k]).wait()

        @pl.loop(0, per // 4)
        def _(i):
            for u in range(4):
                n = i * 4 + u
                t = j * per + n
                x = xs[k, pl.ds(pl.multiple_of(cols[t] * tile, tile), tile), :]
                acc[rows[t]] += jnp.dot(vals[k, n], x, preferred_element_type=F32)

    for k in range(N):
        first = target(c, k) * 2 * pieces
        for p in range(pieces):
            theirs[k, p * tile : (p + 1) * tile, :] = acc[first + (1 - core) * pieces + p].astype(BF16)
            mine[k][p * tile : (p + 1) * tile, :] = acc[first + core * pieces + p]


def backward_kernel(here, rows, cols, values, grads, *refs):
    outs = refs[:N]
    vals, gs, acc, vsem, gsem = refs[N:]
    s = here[0]
    per = values.shape[0] // N
    tile = values.shape[1]
    pieces = acc.shape[1] - 1
    pltpu.make_async_copy(grads, gs, gsem).start()
    for k in range(N):
        j = target(s, k)
        pltpu.make_async_copy(values.at[pl.ds(j * per, per)], vals.at[k], vsem.at[k]).start()
    acc[...] = jnp.zeros_like(acc)
    pltpu.make_async_copy(grads, gs, gsem).wait()
    for k in range(N):
        j = target(s, k)
        pltpu.make_async_copy(values.at[pl.ds(j * per, per)], vals.at[k], vsem.at[k]).wait()

        @pl.loop(0, per // 4)
        def _(i):
            for u in range(4):
                n = i * 4 + u
                t = j * per + n
                g = gs[pl.ds(pl.multiple_of(rows[t] * tile, tile), tile), :]
                acc[k, cols[t]] += lax.dot_general(
                    vals[k, n], g, (((0,), (0,)), ((), ())), preferred_element_type=F32
                )

        for p in range(pieces):
            outs[k][p * tile : (p + 1) * tile, :] = acc[k, p].astype(BF16)


def dense_kernel(*refs):
    parts, (cot, weight), (act, agg_grad, term) = refs[:N], refs[N : N + 2], refs[N + 2 :]
    agg = parts[0][...].astype(F32)
    for part in parts[1:]:
        agg = agg + part[...].astype(F32)
    low = agg.astype(BF16)
    pre = jnp.dot(low, weight[...], preferred_element_type=F32)
    root = 0.7978845608028654
    square = pre * pre
    t = jnp.tanh(root * pre * (1.0 + 0.044715 * square))
    act[...] = (0.5 * pre * (1.0 + t)).astype(BF16)
    slope = 0.5 * (1.0 + t) + 0.5 * pre * (1.0 - t * t) * (root * (1.0 + 3.0 * 0.044715 * square))
    pre_grad = (cot[...].astype(F32) * slope).astype(BF16)
    term[...] = lax.dot_general(low, pre_grad, (((0,), (0,)), ((), ())), preferred_element_type=F32)
    agg_grad[...] = lax.dot_general(
        pre_grad, weight[...], (((1,), (1,)), ((), ())), preferred_element_type=F32
    ).astype(BF16)


def finish_kernel(order, *refs):
    parts, out = refs[:N], refs[N]
    total = parts[0][...].astype(F32)
    for part in parts[1:]:
        total = total + part[...].astype(F32)
    blk = total.shape[0]
    place = lax.broadcasted_iota(jnp.int32, (blk, blk), 0) == order[...]
    out[...] = jnp.dot(place.astype(BF16), total.astype(BF16), preferred_element_type=F32).astype(BF16)


def reorder_kernel(order, features, out):
    blk = features.shape[0]
    pick = lax.broadcasted_iota(jnp.int32, (blk, blk), 0) == order[...]
    out[...] = lax.dot_general(
        pick.astype(BF16), features[...], (((0,), (0,)), ((), ())), preferred_element_type=F32
    ).astype(BF16)


VMEM = pl.BlockSpec(memory_space=pltpu.VMEM)
SMEM = pl.BlockSpec(memory_space=pltpu.SMEM)
ANY = pl.BlockSpec(memory_space=pl.ANY)
MIB = 1 << 20


def shards(features, order, tile_rows, tile_cols, tile_live, tile_values, weight, cotangent):
    blk, width = features.shape
    tile = tile_values.shape[-1]
    pieces = blk // tile
    values = tile_values[0, 0]
    per = values.shape[0] // N
    s = lax.axis_index("section")
    d = lax.axis_index("dom")
    here = jnp.stack([s, d >> 1, d & 1]).astype(jnp.int32)
    live = tile_live[0, 0] != 0
    rows, cols = tile_rows[0, 0], tile_cols[0, 0]
    live_rows = jnp.where(live, rows, 2 * N * pieces)
    block = jax.ShapeDtypeStruct((blk, width), BF16)
    wide = jax.ShapeDtypeStruct((blk, width), F32)

    reordered = pl.pallas_call(
        reorder_kernel, out_shape=block, in_specs=[VMEM] * 2, out_specs=VMEM, name="reorder"
    )(order, features)
    blocks = [reordered] + [to_section(reordered, k) for k in range(1, N)]

    theirs, *mine = pl.pallas_call(
        forward_kernel,
        out_shape=[jax.ShapeDtypeStruct((N, blk, width), BF16)] + [wide] * N,
        in_specs=[SMEM] * 3 + [ANY] * (N + 1),
        out_specs=[VMEM] * (N + 1),
        scratch_shapes=[
            pltpu.VMEM((N, per, tile, tile), BF16),
            pltpu.VMEM((N, blk, width), BF16),
            pltpu.VMEM((2 * N * pieces + 1, tile, width), F32),
            pltpu.SemaphoreType.DMA((N,)),
            pltpu.SemaphoreType.DMA((N,)),
        ],
        compiler_params=pltpu.CompilerParams(vmem_limit_bytes=40 * MIB),
        name="aggregate",
    )(here, live_rows, cols, values, *blocks)

    other = to_core(theirs)
    sums = [(mine[k] + other[k].astype(F32)).astype(BF16) for k in range(N)]
    arrived = [sums[0]] + [to_chip(sums[k], k) for k in range(1, N)]

    activated, agg_grad, term = pl.pallas_call(
        dense_kernel,
        out_shape=[block, block, jax.ShapeDtypeStruct((width, width), F32)],
        in_specs=[VMEM] * (N + 2),
        out_specs=[VMEM] * 3,
        compiler_params=pltpu.CompilerParams(vmem_limit_bytes=24 * MIB),
        name="dense",
    )(*arrived, cotangent, weight)
    panel = lax.all_gather(agg_grad, "dom", axis=0, tiled=True)

    c = d >> 1
    part = width // N

    def cut(k):
        return lax.dynamic_slice_in_dim(term, target(c, k) * part, part)

    own = cut(0)
    for k in range(1, N):
        own = own + to_chip(cut(k), k)
    own = own + to_core(own)
    total = own
    for k in range(1, N):
        total = total + to_section(own, k)
    weight_grad = jnp.zeros((width, width), F32)
    for k in range(N):
        got = total if k == 0 else to_chip(total, k)
        weight_grad = lax.dynamic_update_slice_in_dim(weight_grad, got, source(c, k) * part, 0)

    back_cols = jnp.where(live, cols, pieces)
    outs = pl.pallas_call(
        backward_kernel,
        out_shape=[block] * N,
        in_specs=[SMEM] * 3 + [ANY] * 2,
        out_specs=[VMEM] * N,
        scratch_shapes=[
            pltpu.VMEM((N, per, tile, tile), BF16),
            pltpu.VMEM((2 * N * blk, width), BF16),
            pltpu.VMEM((N, pieces + 1, tile, width), F32),
            pltpu.SemaphoreType.DMA((N,)),
            pltpu.SemaphoreType.DMA,
        ],
        compiler_params=pltpu.CompilerParams(vmem_limit_bytes=40 * MIB),
        name="aggregate_back",
    )(here, rows, back_cols, values, panel)
    pieces_back = [outs[0]] + [to_section(outs[k], k) for k in range(1, N)]
    feature_grad = pl.pallas_call(
        finish_kernel,
        out_shape=block,
        in_specs=[VMEM] * (N + 1),
        out_specs=VMEM,
        compiler_params=pltpu.CompilerParams(vmem_limit_bytes=24 * MIB),
        name="finish",
    )(order, *pieces_back)
    return (activated, feature_grad, weight_grad)


def solution(mesh):
    return jax.shard_map(
        shards,
        mesh=mesh,
        in_specs=(
            P(("section", "dom"), None),
            P(("section", "dom"), None),
            P("section", "dom", None),
            P("section", "dom", None),
            P("section", "dom", None),
            P("section", "dom", None, None, None),
            P(),
            P(("section", "dom"), None),
        ),
        out_specs=(P(("section", "dom"), None), P(("section", "dom"), None), P()),
        check_vma=False,
    )
```

```python
import functools

import jax
import jax.numpy as jnp
from jax import lax
from jax.experimental import pallas as pl
from jax.experimental.pallas import tpu as pltpu
from jax.sharding import PartitionSpec as P

F32 = jnp.float32
BF16 = jnp.bfloat16
N = 8
GROUP = 8
LIST = 128
NEAR, FAR = (4, 1, 3, 2, 0), (5, 7, 6)
ORDER = (4, 6, 5, 7, 2, 1, 3, 0)


def target(i, k):
    return ((i >> 2) ^ (k >> 2)) * 4 + ((i + k) & 3)


def source(i, k):
    return ((i >> 2) ^ (k >> 2)) * 4 + ((i - k) & 3)


def offset(i, j):
    return ((i >> 2) ^ (j >> 2)) * 4 + ((i - j) & 3)


def to_section(x, k):
    return lax.ppermute(x, "section", [(i, target(i, k)) for i in range(N)])


def to_chip(x, k):
    return lax.ppermute(x, "dom", [(2 * i + q, 2 * target(i, k) + q) for i in range(N) for q in range(2)])


def to_core(x):
    return lax.ppermute(x, "dom", [(d, d ^ 1) for d in range(2 * N)])


def look(k, lists):
    which, rank = jnp.int32(0), jnp.int32(0)
    for n, slots in enumerate(lists):
        for m, slot in enumerate(slots):
            which, rank = jnp.where(k == slot, n, which), jnp.where(k == slot, m, rank)
    return which, rank


def halves(order):
    return order[: N // 2], order[N // 2 :]


def list_tiles(tiles, jobs, lists, where, whole, pieces, spare):
    per = tiles.shape[0] // N
    for n in range(2):
        jobs[2 * LIST + n] = 0

    @pl.loop(0, N)
    def _(j):
        a, rank = look(where(j), lists)
        base = a * LIST

        def one(i, n):
            word = tiles[j * per + i]
            first = j * per + i if whole else i
            jobs[base + n] = (first << 16) | (word & 0xFF00) | (rank * pieces + (word & 255))
            return n + (word >> 16)

        jobs[2 * LIST + a] = lax.fori_loop(0, per, one, jobs[2 * LIST + a], unroll=True)

    for n in range(2):
        for i in range(GROUP):
            jobs[n * LIST + jobs[2 * LIST + n] + i] = spare


def prepare_kernel(here, tiles, values, after, kept, acc, jobs, sem):
    del after
    copy = pltpu.make_async_copy(values, kept, sem)
    copy.start()
    acc[...] = jnp.zeros_like(acc)
    s = here[0]
    total = acc.shape[0] - 1
    lists = (NEAR, FAR)
    list_tiles(tiles, jobs, lists, lambda j: offset(s, j), True, total // (2 * N), total << 8)
    copy.wait()


def prepare_back_kernel(pieces, here, tiles, after, jobs):
    del after
    s = here[0]
    list_tiles(tiles, jobs, halves(ORDER), lambda j: offset(j, s), False, pieces, 4 * pieces)


def run_jobs(which, jobs, body):
    @pl.loop(0, (jobs[2 * LIST + which] + GROUP - 1) // GROUP)
    def _(i):
        for u in range(GROUP):
            job = jobs[which * LIST + i * GROUP + u]
            body(job >> 16, (job >> 8) & 255, job & 255)


def place(blocks, buffer, sem):
    copies = [pltpu.make_async_copy(ref, buffer.at[n], sem.at[n]) for n, ref in enumerate(blocks)]
    for copy in copies:
        copy.start()
    for copy in copies:
        copy.wait()


def near_kernel(jobs, values, before, *refs):
    del before
    blocks, (acc, xs, sem) = refs[:-3], refs[-3:]
    place(blocks, xs, sem)
    multiply(0, jobs, values, xs, acc)


def multiply(which, jobs, values, xs, acc):
    tile = values.shape[1]
    pieces = xs.shape[1] // tile

    def body(t, r, x):
        block = xs[x // pieces, pl.ds(pl.multiple_of((x % pieces) * tile, tile), tile), :]
        acc[r] += jnp.dot(values[t], block, preferred_element_type=F32)

    run_jobs(which, jobs, body)


def far_kernel(here, jobs, values, before, *refs):
    del before
    blocks, (acc, theirs, xs, sem) = refs[:-4], refs[-4:]
    place(blocks, xs, sem)
    multiply(1, jobs, values, xs, acc)
    tile = values.shape[1]
    pieces = xs.shape[1] // tile
    for k in range(N):
        first = (target(here[1], k) * 2 + 1 - here[2]) * pieces
        for p in range(pieces):
            theirs[k, p * tile : (p + 1) * tile, :] = acc[first + p].astype(BF16)


def pair_kernel(here, acc, other, *outs):
    tile = acc.shape[1]
    pieces = other.shape[1] // tile
    for k, out in enumerate(outs):
        first = (target(here[1], k) * 2 + here[2]) * pieces
        for p in range(pieces):
            rows = slice(p * tile, (p + 1) * tile)
            out[rows, :] = (acc[first + p] + other[k, rows, :].astype(F32)).astype(BF16)


def back_kernel(here, jobs, values, panel, w, *refs):
    outs, (vals, gs, acc, sem) = refs[:-4], refs[-4:]
    per, tile = vals.shape[1], vals.shape[2]
    blk = gs.shape[1]
    pieces = blk // tile
    copies = [
        pltpu.make_async_copy(values.at[pl.ds(target(here[0], k) * per, per)], vals.at[n], sem.at[n])
        for n, k in enumerate(ORDER)
    ]
    copies.insert(0, pltpu.make_async_copy(panel, gs, sem.at[N]))
    for copy in copies:
        copy.start()
    acc[...] = jnp.zeros_like(acc)
    high = w[...].astype(BF16)
    low = (w[...] - high.astype(F32)).astype(BF16)
    part = high.shape[0]
    for out in outs:
        out[blk : blk + part, :] = high
        out[blk + part :, :] = low
    for which in range(2):
        first = which * (N // 2)
        for copy in copies[first + which : first + N // 2 + 1]:
            copy.wait()

        def body(t, g, q):
            block = gs[g // pieces, pl.ds(pl.multiple_of((g % pieces) * tile, tile), tile), :]
            near = vals[first + jnp.minimum(q // pieces, N // 2 - 1), t]
            acc[first * pieces + which + q] += lax.dot_general(
                near, block, (((0,), (0,)), ((), ())), preferred_element_type=F32
            )

        run_jobs(which, jobs, body)
        for k in range(N // 2):
            for p in range(pieces):
                outs[first + k][p * tile : (p + 1) * tile, :] = acc[(first + k) * pieces + which + p].astype(BF16)


def dense_kernel(*refs):
    parts, (cot, weight), (act, agg_grad, term) = refs[:N], refs[N : N + 2], refs[N + 2 :]
    agg = parts[0][...].astype(F32)
    for part in parts[1:]:
        agg = agg + part[...].astype(F32)
    low = agg.astype(BF16)
    pre = jnp.dot(low, weight[...], preferred_element_type=F32)
    root = 0.7978845608028654
    square = pre * pre
    t = jnp.tanh(root * pre * (1.0 + 0.044715 * square))
    act[...] = (0.5 * pre * (1.0 + t)).astype(BF16)
    slope = 0.5 * (1.0 + t) + 0.5 * pre * (1.0 - t * t) * (root * (1.0 + 3.0 * 0.044715 * square))
    pre_grad = (cot[...].astype(F32) * slope).astype(BF16)
    term[...] = lax.dot_general(low, pre_grad, (((0,), (0,)), ((), ())), preferred_element_type=F32)
    agg_grad[...] = lax.dot_general(
        pre_grad, weight[...], (((1,), (1,)), ((), ())), preferred_element_type=F32
    ).astype(BF16)


def finish_kernel(here, order, w, *refs):
    parts, (out, grad) = refs[:N], refs[N:]
    blk = out.shape[0]
    part = w.shape[0]
    total = parts[0][:blk, :].astype(F32)
    for n, k in enumerate(ORDER):
        if n:
            total = total + parts[n][:blk, :].astype(F32)
        rows = parts[n][blk : blk + part, :].astype(F32) + parts[n][blk + part :, :].astype(F32)
        grad[pl.ds(pl.multiple_of(source(here[0], k) * part, part), part), :] = w[...] if k == 0 else rows
    place = lax.broadcasted_iota(jnp.int32, (blk, blk), 0) == order[...]
    out[...] = jnp.dot(place.astype(BF16), total.astype(BF16), preferred_element_type=F32).astype(BF16)


def reorder_kernel(order, features, out):
    blk = features.shape[0]
    pick = lax.broadcasted_iota(jnp.int32, (blk, blk), 0) == order[...]
    out[...] = lax.dot_general(
        pick.astype(BF16), features[...], (((0,), (0,)), ((), ())), preferred_element_type=F32
    ).astype(BF16)


VMEM = pl.BlockSpec(memory_space=pltpu.VMEM)
SMEM = pl.BlockSpec(memory_space=pltpu.SMEM)
HBM = pl.BlockSpec(memory_space=pltpu.HBM)
MIB = 1 << 20


def shards(features, order, tile_rows, tile_cols, tile_live, tile_values, weight, cotangent):
    blk, width = features.shape
    tile = tile_values.shape[-1]
    pieces = blk // tile
    half = blk // 2
    values = tile_values[0, 0]
    s = lax.axis_index("section")
    d = lax.axis_index("dom")
    c, core = d >> 1, d & 1
    here = jnp.stack([s, c, core]).astype(jnp.int32)
    block = jax.ShapeDtypeStruct((blk, width), BF16)
    held = pltpu.VMEM((blk, width), BF16)
    stack = pltpu.VMEM((2 * N * pieces + 1, tile, width), F32)
    params = pltpu.CompilerParams(vmem_limit_bytes=24 * MIB)

    def together(*arrays):
        return lax.optimization_barrier(arrays)

    reordered = pl.pallas_call(
        reorder_kernel, out_shape=held, in_specs=[VMEM] * 2, out_specs=VMEM, name="reorder"
    )(order, features)
    first = {k: to_section(reordered, k) if k else reordered for k in NEAR}
    tiles = (tile_live[0, 0] << 16) | (tile_rows[0, 0] << 8) | tile_cols[0, 0]
    stored = values
    values, acc, jobs = pl.pallas_call(
        prepare_kernel,
        out_shape=[
            pltpu.VMEM(stored.shape, BF16),
            stack,
            jax.ShapeDtypeStruct((2 * LIST + 2,), jnp.int32),
        ],
        in_specs=[SMEM] * 2 + [HBM, VMEM],
        out_specs=[VMEM] * 2 + [SMEM],
        scratch_shapes=[pltpu.SemaphoreType.DMA],
        compiler_params=pltpu.CompilerParams(vmem_limit_bytes=44 * MIB),
        name="prepare",
    )(here, tiles, stored, reordered)
    first[4], acc = together(first[4], acc)
    second = {k: to_section(first[4], k & 3) for k in FAR}
    flops = 96 * tile * tile * width * 2
    cost = pl.CostEstimate(flops=flops, bytes_accessed=12 * MIB, transcendentals=0)
    acc = pl.pallas_call(
        near_kernel,
        out_shape=stack,
        in_specs=[SMEM] + [VMEM] * (len(NEAR) + 2),
        out_specs=VMEM,
        scratch_shapes=[pltpu.VMEM((len(NEAR), blk, width), BF16), pltpu.SemaphoreType.DMA((len(NEAR),))],
        input_output_aliases={2: 0},
        compiler_params=params,
        cost_estimate=cost,
        name="aggregate_near",
    )(jobs, values, acc, *[first[k] for k in NEAR])
    acc, theirs = pl.pallas_call(
        far_kernel,
        out_shape=[stack, pltpu.VMEM((N, blk, width), BF16)],
        in_specs=[SMEM] * 2 + [VMEM] * (len(FAR) + 2),
        out_specs=[VMEM] * 2,
        scratch_shapes=[pltpu.VMEM((len(FAR), blk, width), BF16), pltpu.SemaphoreType.DMA((len(FAR),))],
        input_output_aliases={3: 0},
        compiler_params=params,
        cost_estimate=cost,
        name="aggregate_far",
    )(here, jobs, values, acc, *[second[k] for k in FAR])
    sums = pl.pallas_call(
        pair_kernel,
        out_shape=[held] * N,
        in_specs=[SMEM] + [VMEM] * 2,
        out_specs=[VMEM] * N,
        compiler_params=params,
        name="pair",
    )(here, acc, to_core(theirs))
    arrived = [to_chip(sums[k], k) if k else sums[k] for k in (1, 3, 6, 5, 7, 4, 2, 0)]

    activated, agg_grad, term = pl.pallas_call(
        dense_kernel,
        out_shape=[block, block, pltpu.VMEM((width, width), F32)],
        in_specs=[VMEM] * (N + 2),
        out_specs=[VMEM] * 3,
        compiler_params=params,
        name="dense",
    )(*arrived, cotangent, weight)

    def swap(x, axis, bit):
        n = lax.axis_size(axis)
        return lax.ppermute(x, axis, [(i, i ^ bit) for i in range(n)])

    def halve(x, bit):
        n = x.shape[0] // 2
        high = (s & bit) != 0
        keep = jnp.where(high, x[n:], x[:n])
        return keep + swap(jnp.where(high, x[:n], x[n:]), "section", bit)

    panel = lax.all_gather(agg_grad, "dom", axis=0)
    w = halve(halve(term, 4), 2)
    jobs = pl.pallas_call(
        functools.partial(prepare_back_kernel, pieces),
        out_shape=jax.ShapeDtypeStruct((2 * LIST + 2,), jnp.int32),
        in_specs=[SMEM] * 2 + [VMEM],
        out_specs=SMEM,
        name="prepare_back",
    )(here, tiles, w)
    w = halve(w, 1)
    jobs, w = together(jobs, w)
    for bit in (8, 4, 2, 1):
        w = w + swap(w, "dom", bit)
    panel, w = together(panel, w)
    message = pltpu.VMEM((blk + 2 * w.shape[0], width), BF16)

    outs = pl.pallas_call(
        back_kernel,
        out_shape=[message] * N,
        in_specs=[SMEM] * 2 + [HBM] * 2 + [VMEM],
        out_specs=[VMEM] * N,
        scratch_shapes=[
            pltpu.VMEM((N, stored.shape[0] // N, tile, tile), BF16),
            pltpu.VMEM(panel.shape, BF16),
            pltpu.VMEM((N * pieces + 2, tile, width), F32),
            pltpu.SemaphoreType.DMA((N + 1,)),
        ],
        compiler_params=pltpu.CompilerParams(vmem_limit_bytes=56 * MIB),
        cost_estimate=cost,
        name="aggregate_back",
    )(here, jobs, stored, panel, w)
    back = [to_section(out, k) if k else out for k, out in zip(ORDER, outs)]
    feature_grad, weight_grad = pl.pallas_call(
        finish_kernel,
        out_shape=[block, jax.ShapeDtypeStruct((width, width), F32)],
        in_specs=[SMEM] + [VMEM] * (N + 2),
        out_specs=[VMEM] * 2,
        compiler_params=params,
        name="finish",
    )(here, order, w, *back)
    return (activated, feature_grad, weight_grad)


def solution(mesh):
    return jax.shard_map(
        shards,
        mesh=mesh,
        in_specs=(
            P(("section", "dom"), None),
            P(("section", "dom"), None),
            P("section", "dom", None),
            P("section", "dom", None),
            P("section", "dom", None),
            P("section", "dom", None, None, None),
            P(),
            P(("section", "dom"), None),
        ),
        out_specs=(P(("section", "dom"), None), P(("section", "dom"), None), P()),
        check_vma=False,
    )
```

```python
import functools

import jax
import jax.numpy as jnp
from jax import lax
from jax.experimental import pallas as pl
from jax.experimental.pallas import tpu as pltpu
from jax.sharding import PartitionSpec as P

F32 = jnp.float32
BF16 = jnp.bfloat16
N = 8
GROUP = 8
LIST = 128
NEAR, FAR = (4, 1, 3, 2, 0), (5, 7, 6)
ORDER = tuple(range(N))


def target(i, k):
    return ((i >> 2) ^ (k >> 2)) * 4 + ((i + k) & 3)


def source(i, k):
    return ((i >> 2) ^ (k >> 2)) * 4 + ((i - k) & 3)


def offset(i, j):
    return ((i >> 2) ^ (j >> 2)) * 4 + ((i - j) & 3)


def to_section(x, k):
    return lax.ppermute(x, "section", [(i, target(i, k)) for i in range(N)])


def to_chip(x, k):
    return lax.ppermute(x, "dom", [(2 * i + q, 2 * target(i, k) + q) for i in range(N) for q in range(2)])


def to_core(x):
    return lax.ppermute(x, "dom", [(d, d ^ 1) for d in range(2 * N)])


def look(k, lists):
    which, rank = jnp.int32(0), jnp.int32(0)
    for n, slots in enumerate(lists):
        for m, slot in enumerate(slots):
            which, rank = jnp.where(k == slot, n, which), jnp.where(k == slot, m, rank)
    return which, rank


def list_tiles(tiles, jobs, lists, where, pieces, spare):
    per = tiles.shape[0] // N
    for n in range(2):
        jobs[2 * LIST + n] = 0

    @pl.loop(0, N)
    def _(j):
        a, rank = look(where(j), lists)
        base = a * LIST

        def one(i, n):
            word = tiles[j * per + i]
            jobs[base + n] = ((j * per + i) << 16) | (word & 0xFF00) | (rank * pieces + (word & 255))
            return n + (word >> 16)

        jobs[2 * LIST + a] = lax.fori_loop(0, per, one, jobs[2 * LIST + a], unroll=True)

    for n in range(len(lists)):
        for i in range(GROUP):
            jobs[n * LIST + jobs[2 * LIST + n] + i] = spare


def prepare_kernel(here, tiles, values, after, kept, acc, jobs, sem):
    del after
    copy = pltpu.make_async_copy(values, kept, sem)
    copy.start()
    acc[...] = jnp.zeros_like(acc)
    s = here[0]
    total = acc.shape[0] - 1
    lists = (NEAR, FAR)
    list_tiles(tiles, jobs, lists, lambda j: offset(s, j), total // (2 * N), total << 8)
    copy.wait()


def prepare_back_kernel(pieces, here, tiles, after, jobs):
    del after
    s = here[0]
    list_tiles(tiles, jobs, (ORDER[: N // 2], ORDER[N // 2 :]), lambda j: offset(j, s), pieces, (N // 2) * pieces)


def run_jobs(which, jobs, body):
    @pl.loop(0, (jobs[2 * LIST + which] + GROUP - 1) // GROUP)
    def _(i):
        for u in range(GROUP):
            job = jobs[which * LIST + i * GROUP + u]
            body(job >> 16, (job >> 8) & 255, job & 255)


def place(blocks, buffer, sem):
    copies = [pltpu.make_async_copy(ref, buffer.at[n], sem.at[n]) for n, ref in enumerate(blocks)]
    for copy in copies:
        copy.start()
    for copy in copies:
        copy.wait()


def near_kernel(jobs, values, before, *refs):
    del before
    blocks, (acc, xs, sem) = refs[:-3], refs[-3:]
    place(blocks, xs, sem)
    multiply(0, jobs, values, xs, acc)


def multiply(which, jobs, values, xs, acc):
    tile = values.shape[1]
    pieces = xs.shape[1] // tile

    def body(t, r, x):
        block = xs[x // pieces, pl.ds(pl.multiple_of((x % pieces) * tile, tile), tile), :]
        acc[r] += jnp.dot(values[t], block, preferred_element_type=F32)

    run_jobs(which, jobs, body)


def far_kernel(here, jobs, values, before, *refs):
    del before
    blocks, (acc, across, along, xs, sem) = refs[:-5], refs[-5:]
    place(blocks, xs, sem)
    multiply(1, jobs, values, xs, acc)
    tile = values.shape[1]
    pieces = xs.shape[1] // tile
    for k in range(N):
        first = (target(here[1], k) * 2 + 1 - here[2]) * pieces
        theirs = across if k >= N // 2 else along
        for p in range(pieces):
            theirs[k % (N // 2), p * tile : (p + 1) * tile, :] = acc[first + p].astype(BF16)


def pair_kernel(start, here, acc, other, *outs):
    tile = acc.shape[1]
    pieces = other.shape[1] // tile
    for n, out in enumerate(outs):
        k = start + n
        first = (target(here[1], k) * 2 + here[2]) * pieces
        for p in range(pieces):
            rows = slice(p * tile, (p + 1) * tile)
            out[rows, :] = (acc[first + p] + other[n, rows, :].astype(F32)).astype(BF16)


def back_kernel(here, jobs, values, panel, w, x1, x2, x3, y1, x0, y0, vals, gs, acc, sem):
    per, tile = vals.shape[0] // N, vals.shape[1]
    pieces = gs.shape[1] // tile
    half = pieces // 2
    copies = [pltpu.make_async_copy(panel, gs, sem.at[N])]
    for k in ORDER:
        rows = pl.ds(target(here[0], k) * per, per)
        copies.append(pltpu.make_async_copy(values.at[rows], vals.at[rows], sem.at[k]))
    for copy in copies:
        copy.start()
    acc[...] = jnp.zeros_like(acc)
    xs = (x0, x1, x2, x3)
    for out in xs[1:]:
        out[2 * half * tile :, :] = w[...].astype(BF16)
    for high in range(2):
        for copy in copies[5:] if high else copies[:5]:
            copy.wait()
        base = high * (4 * pieces + 1)

        def body(t, g, q):
            block = gs[g // pieces, pl.ds(pl.multiple_of((g % pieces) * tile, tile), tile), :]
            acc[base + q] += lax.dot_general(vals[t], block, (((0,), (0,)), ((), ())), preferred_element_type=F32)

        run_jobs(high, jobs, body)
        y = (y0, y1)[high]
        for b in range(4):
            for p in range(half):
                out, row = xs[b], (high * half + p) * tile
                out[row : row + tile, :] = acc[base + b * pieces + p].astype(out.dtype)
                row = (b * half + p) * tile
                y[row : row + tile, :] = acc[base + b * pieces + half + p].astype(y.dtype)


def middle_kernel(w, x0, y0, x1, x2, x3, y1, message, z1, z2, z3, top, low):
    rows = top.shape[0]
    message[rows : rows + w.shape[0], :] = w[...].astype(BF16)
    for b, x in enumerate((x1, x2, x3), 1):
        at = rows + b * w.shape[0]
        message[at : at + w.shape[0], :] = x[2 * rows :, :]
    sums = x0[...]
    for x in (x1, x2, x3):
        sums = sums + x[: 2 * rows, :].astype(F32)
    top[...] = sums[:rows, :]
    message[:rows, :] = sums[rows:, :].astype(BF16)
    for b, z in enumerate((low, z1, z2, z3)):
        at = slice(b * rows, (b + 1) * rows)
        z[...] = (y0[at, :] + y1[at, :].astype(F32)).astype(z.dtype)


def dense_kernel(*refs):
    parts, (cot, weight), (act, agg_grad, term) = refs[:N], refs[N : N + 2], refs[N + 2 :]
    agg = parts[0][...].astype(F32)
    for part in parts[1:]:
        agg = agg + part[...].astype(F32)
    low = agg.astype(BF16)
    pre = jnp.dot(low, weight[...], preferred_element_type=F32)
    root = 0.7978845608028654
    square = pre * pre
    t = jnp.tanh(root * pre * (1.0 + 0.044715 * square))
    act[...] = (0.5 * pre * (1.0 + t)).astype(BF16)
    slope = 0.5 * (1.0 + t) + 0.5 * pre * (1.0 - t * t) * (root * (1.0 + 3.0 * 0.044715 * square))
    pre_grad = (cot[...].astype(F32) * slope).astype(BF16)
    term[...] = lax.dot_general(low, pre_grad, (((0,), (0,)), ((), ())), preferred_element_type=F32)
    agg_grad[...] = lax.dot_general(
        pre_grad, weight[...], (((1,), (1,)), ((), ())), preferred_element_type=F32
    ).astype(BF16)


def finish_kernel(here, order, own, got, top, low, z1, z2, z3, out, grad):
    rows = top.shape[0]
    part = grad.shape[0] // N
    for high, message in enumerate((own, got)):
        for b in range(4):
            at = pl.multiple_of(source(here[0], high * 4 + b) * part, part)
            grad[pl.ds(at, part), :] = message[rows + b * part : rows + (b + 1) * part, :].astype(F32)
    upper = (top[...] + got[:rows, :].astype(F32)).astype(BF16)
    lower = low[...]
    for z in (z1, z2, z3):
        lower = lower + z[...].astype(F32)
    total = jnp.concatenate([upper, lower.astype(BF16)], axis=0)
    blk = total.shape[0]
    place = lax.broadcasted_iota(jnp.int32, (blk, blk), 0) == order[...]
    out[...] = jnp.dot(place.astype(BF16), total, preferred_element_type=F32).astype(BF16)


def reorder_kernel(order, features, out):
    blk = features.shape[0]
    pick = lax.broadcasted_iota(jnp.int32, (blk, blk), 0) == order[...]
    out[...] = lax.dot_general(
        pick.astype(BF16), features[...], (((0,), (0,)), ((), ())), preferred_element_type=F32
    ).astype(BF16)


VMEM = pl.BlockSpec(memory_space=pltpu.VMEM)
SMEM = pl.BlockSpec(memory_space=pltpu.SMEM)
HBM = pl.BlockSpec(memory_space=pltpu.HBM)
MIB = 1 << 20


def shards(features, order, tile_rows, tile_cols, tile_live, tile_values, weight, cotangent):
    blk, width = features.shape
    tile = tile_values.shape[-1]
    pieces = blk // tile
    half = blk // 2
    values = tile_values[0, 0]
    s = lax.axis_index("section")
    d = lax.axis_index("dom")
    c, core = d >> 1, d & 1
    here = jnp.stack([s, c, core]).astype(jnp.int32)
    block = jax.ShapeDtypeStruct((blk, width), BF16)
    held = pltpu.VMEM((blk, width), BF16)
    stack = pltpu.VMEM((2 * N * pieces + 1, tile, width), F32)
    params = pltpu.CompilerParams(vmem_limit_bytes=24 * MIB)

    def together(*arrays):
        return lax.optimization_barrier(arrays)

    reordered = pl.pallas_call(
        reorder_kernel, out_shape=held, in_specs=[VMEM] * 2, out_specs=VMEM, name="reorder"
    )(order, features)
    first = {k: to_section(reordered, k) if k else reordered for k in NEAR}
    tiles = (tile_live[0, 0] << 16) | (tile_rows[0, 0] << 8) | tile_cols[0, 0]
    stored = values
    values, acc, jobs = pl.pallas_call(
        prepare_kernel,
        out_shape=[
            pltpu.VMEM(stored.shape, BF16),
            stack,
            jax.ShapeDtypeStruct((2 * LIST + 2,), jnp.int32),
        ],
        in_specs=[SMEM] * 2 + [HBM, VMEM],
        out_specs=[VMEM] * 2 + [SMEM],
        scratch_shapes=[pltpu.SemaphoreType.DMA],
        compiler_params=pltpu.CompilerParams(vmem_limit_bytes=44 * MIB),
        name="prepare",
    )(here, tiles, stored, reordered)
    first[4], acc = together(first[4], acc)
    second = {k: to_section(first[4], k & 3) for k in FAR}
    flops = 96 * tile * tile * width * 2
    cost = pl.CostEstimate(flops=flops, bytes_accessed=12 * MIB, transcendentals=0)
    acc = pl.pallas_call(
        near_kernel,
        out_shape=stack,
        in_specs=[SMEM] + [VMEM] * (len(NEAR) + 2),
        out_specs=VMEM,
        scratch_shapes=[pltpu.VMEM((len(NEAR), blk, width), BF16), pltpu.SemaphoreType.DMA((len(NEAR),))],
        input_output_aliases={2: 0},
        compiler_params=params,
        cost_estimate=cost,
        name="aggregate_near",
    )(jobs, values, acc, *[first[k] for k in NEAR])
    four = pltpu.VMEM((N // 2, blk, width), BF16)
    acc, across, along = pl.pallas_call(
        far_kernel,
        out_shape=[stack, four, four],
        in_specs=[SMEM] * 2 + [VMEM] * (len(FAR) + 2),
        out_specs=[VMEM] * 3,
        scratch_shapes=[pltpu.VMEM((len(FAR), blk, width), BF16), pltpu.SemaphoreType.DMA((len(FAR),))],
        input_output_aliases={3: 0},
        compiler_params=params,
        cost_estimate=cost,
        name="aggregate_far",
    )(here, jobs, values, acc, *[second[k] for k in FAR])

    def pair_sums(start, other):
        return pl.pallas_call(
            functools.partial(pair_kernel, start),
            out_shape=[held] * (N // 2),
            in_specs=[SMEM] + [VMEM] * 2,
            out_specs=[VMEM] * (N // 2),
            compiler_params=params,
            name=f"pair_{start}",
        )(here, acc, other)

    across, along = to_core(across), to_core(along)
    far_sums = pair_sums(N // 2, across)
    near_sums = pair_sums(0, along)
    sums = [*near_sums, *far_sums]
    arrived = [to_chip(sums[k], k) if k else sums[k] for k in (1, 3, 6, 5, 7, 4, 2, 0)]

    activated, agg_grad, term = pl.pallas_call(
        dense_kernel,
        out_shape=[block, block, pltpu.VMEM((width, width), F32)],
        in_specs=[VMEM] * (N + 2),
        out_specs=[VMEM] * 3,
        compiler_params=params,
        name="dense",
    )(*arrived, cotangent, weight)

    def swap(x, axis, bit):
        n = lax.axis_size(axis)
        return lax.ppermute(x, axis, [(i, i ^ bit) for i in range(n)])

    def halve(x, bit):
        n = x.shape[0] // 2
        high = (s & bit) != 0
        keep = jnp.where(high, x[n:], x[:n])
        return keep + swap(jnp.where(high, x[:n], x[n:]), "section", bit)

    panel = lax.all_gather(agg_grad, "dom", axis=0)
    w = halve(halve(term, 4), 2)
    jobs = pl.pallas_call(
        functools.partial(prepare_back_kernel, pieces),
        out_shape=jax.ShapeDtypeStruct((2 * LIST + 2,), jnp.int32),
        in_specs=[SMEM] * 2 + [VMEM],
        out_specs=SMEM,
        name="prepare_back",
    )(here, tiles, w)
    w = halve(w, 1)
    jobs, w = together(jobs, w)
    for bit in (8, 4, 2, 1):
        w = w + swap(w, "dom", bit)
    panel, w = together(panel, w)
    part = w.shape[0]

    def wide(rows, dtype=BF16):
        return pltpu.VMEM((rows, width), dtype)

    x1, x2, x3, y1, x0, y0 = pl.pallas_call(
        back_kernel,
        out_shape=[wide(blk + part)] * 3 + [wide(2 * blk), wide(blk, F32), wide(2 * blk, F32)],
        in_specs=[SMEM] * 2 + [HBM] * 2 + [VMEM],
        out_specs=[VMEM] * 6,
        scratch_shapes=[
            pltpu.VMEM(stored.shape, BF16),
            pltpu.VMEM(panel.shape, BF16),
            pltpu.VMEM((N * pieces + 2, tile, width), F32),
            pltpu.SemaphoreType.DMA((N + 1,)),
        ],
        compiler_params=pltpu.CompilerParams(vmem_limit_bytes=56 * MIB),
        cost_estimate=cost,
        name="aggregate_back",
    )(here, jobs, stored, panel, w)
    message, z1, z2, z3, top, low = pl.pallas_call(
        middle_kernel,
        out_shape=[wide(half + 4 * part)] + [wide(half)] * 3 + [wide(half, F32)] * 2,
        in_specs=[VMEM] * 7,
        out_specs=[VMEM] * 6,
        compiler_params=params,
        name="middle",
    )(w, x0, y0, to_section(x1, 1), to_section(x2, 2), to_section(x3, 3), to_section(y1, 4))
    feature_grad, weight_grad = pl.pallas_call(
        finish_kernel,
        out_shape=[block, jax.ShapeDtypeStruct((width, width), F32)],
        in_specs=[SMEM] + [VMEM] * 8,
        out_specs=[VMEM] * 2,
        compiler_params=params,
        name="finish",
    )(
        here, order, message, to_section(message, 4), top, low, to_section(z1, 1), to_section(z2, 2), to_section(z3, 3)
    )
    return (activated, feature_grad, weight_grad)


def solution(mesh):
    return jax.shard_map(
        shards,
        mesh=mesh,
        in_specs=(
            P(("section", "dom"), None),
            P(("section", "dom"), None),
            P("section", "dom", None),
            P("section", "dom", None),
            P("section", "dom", None),
            P("section", "dom", None, None, None),
            P(),
            P(("section", "dom"), None),
        ),
        out_specs=(P(("section", "dom"), None), P(("section", "dom"), None), P()),
        check_vma=False,
    )
```

```python
import functools

import jax
import jax.numpy as jnp
from jax import lax
from jax.experimental import pallas as pl
from jax.experimental.pallas import tpu as pltpu
from jax.sharding import PartitionSpec as P

F32 = jnp.float32
BF16 = jnp.bfloat16
N = 8
GROUP = 8
PAIRS = 4
LIST = 128
NEAR, FAR = (4, 1, 3, 2, 0), (5, 7, 6)
ORDER = tuple(range(N))


def target(i, k):
    return ((i >> 2) ^ (k >> 2)) * 4 + ((i + k) & 3)


def source(i, k):
    return ((i >> 2) ^ (k >> 2)) * 4 + ((i - k) & 3)


def offset(i, j):
    return ((i >> 2) ^ (j >> 2)) * 4 + ((i - j) & 3)


def to_section(x, k):
    return lax.ppermute(x, "section", [(i, target(i, k)) for i in range(N)])


def to_chip(x, k):
    return lax.ppermute(x, "dom", [(2 * i + q, 2 * target(i, k) + q) for i in range(N) for q in range(2)])


def to_core(x):
    return lax.ppermute(x, "dom", [(d, d ^ 1) for d in range(2 * N)])


def position():
    d = lax.axis_index("dom")
    return lax.axis_index("section"), d >> 1, d & 1


def look(k, lists):
    which, rank = jnp.int32(0), jnp.int32(0)
    for n, slots in enumerate(lists):
        for m, slot in enumerate(slots):
            which, rank = jnp.where(k == slot, n, which), jnp.where(k == slot, m, rank)
    return which, rank


def list_tiles(tiles, jobs, lists, where, pieces, spare):
    per = tiles.shape[0] // N
    for n in range(2):
        jobs[2 * LIST + n] = 0

    @pl.loop(0, N)
    def _(j):
        a, rank = look(where(j), lists)
        base = a * LIST

        def one(i, n):
            word = tiles[j * per + i]
            jobs[base + n] = ((j * per + i) << 16) | (word & 0xFF00) | (rank * pieces + (word & 255))
            return n + (word >> 16)

        jobs[2 * LIST + a] = lax.fori_loop(0, per, one, jobs[2 * LIST + a], unroll=True)

    for n in range(len(lists)):
        for i in range(GROUP):
            jobs[n * LIST + jobs[2 * LIST + n] + i] = spare


def prepare_kernel(tiles, values, block, kept, acc, jobs, own, sem):
    copies = [pltpu.make_async_copy(values, kept, sem.at[0]), pltpu.make_async_copy(block, own, sem.at[1])]
    for copy in copies:
        copy.start()
    acc[...] = jnp.zeros_like(acc)
    s, _, _ = position()
    total = acc.shape[0] - 1
    lists = (NEAR, FAR)
    list_tiles(tiles, jobs, lists, lambda j: offset(s, j), total // (2 * N), total << 8)
    for copy in copies:
        copy.wait()


def prepare_back_kernel(pieces, tiles, after, jobs, groups, lengths):
    del after
    s, _, _ = position()
    per = tiles.shape[0] // N
    zero = tiles.shape[0] << 16
    sums = N * pieces
    for q in range(sums):
        lengths[q] = 0

    @pl.loop(0, N)
    def _(j):
        k = offset(j, s)

        def one(i, carry):
            word = tiles[j * per + i]
            col = word & 255
            q = k * pieces + col
            n = lengths[q]
            groups[q * per + n] = ((j * per + i) << 16) | (word & 0xFF00) | (q % (sums // 2))
            lengths[q] = n + (word >> 16)
            return carry

        lax.fori_loop(0, per, one, 0, unroll=True)

    for high in range(2):

        def group(q, done):
            n = lengths[q]

            @pl.when(n & 1 == 1)
            def _():
                groups[q * per + n] = zero

            def pair(i, carry):
                for u in range(2):
                    jobs[high * LIST + 2 * (done + i) + u] = groups[q * per + 2 * i + u]
                return carry

            count = (n + 1) >> 1
            lax.fori_loop(0, count, pair, 0)
            return done + count

        done = lax.fori_loop(high * (sums // 2), (high + 1) * (sums // 2), group, jnp.int32(0))
        jobs[2 * LIST + high] = done
        for i in range(2 * PAIRS):
            jobs[high * LIST + 2 * done + i] = zero | (sums // 2)


def run_pairs(which, jobs, body):
    @pl.loop(0, (jobs[2 * LIST + which] + PAIRS - 1) // PAIRS)
    def _(i):
        for u in range(PAIRS):
            at = which * LIST + 2 * (i * PAIRS + u)
            a, b = jobs[at], jobs[at + 1]
            body(a & 255, a >> 16, (a >> 8) & 255, b >> 16, (b >> 8) & 255)


def run_jobs(which, jobs, body):
    @pl.loop(0, (jobs[2 * LIST + which] + GROUP - 1) // GROUP)
    def _(i):
        for u in range(GROUP):
            job = jobs[which * LIST + i * GROUP + u]
            body(job >> 16, (job >> 8) & 255, job & 255)


def place(blocks, buffer, sem):
    copies = [pltpu.make_async_copy(ref, buffer.at[n], sem.at[n]) for n, ref in enumerate(blocks)]
    for copy in copies:
        copy.start()
    for copy in copies:
        copy.wait()


def near_kernel(jobs, values, before, *refs):
    del before
    blocks, (acc, xs, sem) = refs[:-3], refs[-3:]
    place(blocks, xs, sem)
    multiply(0, jobs, values, xs, acc)


def multiply(which, jobs, values, xs, acc):
    tile = values.shape[1]
    pieces = xs.shape[1] // tile

    def body(t, r, x):
        block = xs[x // pieces, pl.ds(pl.multiple_of((x % pieces) * tile, tile), tile), :]
        acc[r] += jnp.dot(values[t], block, preferred_element_type=F32)

    run_jobs(which, jobs, body)


def far_kernel(jobs, values, before, *refs):
    del before
    blocks, (acc, across, along, xs, sem) = refs[:-5], refs[-5:]
    place(blocks, xs, sem)
    multiply(1, jobs, values, xs, acc)
    tile = values.shape[1]
    pieces = xs.shape[1] // tile
    _, c, core = position()
    for k in range(N):
        first = (target(c, k) * 2 + 1 - core) * pieces
        theirs = across if k >= N // 2 else along
        for p in range(pieces):
            theirs[k % (N // 2), p * tile : (p + 1) * tile, :] = acc[first + p].astype(BF16)


def pair_kernel(start, acc, other, *outs):
    tile = acc.shape[1]
    pieces = other.shape[1] // tile
    _, c, core = position()
    for n, out in enumerate(outs):
        k = start + n
        first = (target(c, k) * 2 + core) * pieces
        for p in range(pieces):
            rows = slice(p * tile, (p + 1) * tile)
            out[rows, :] = (acc[first + p] + other[n, rows, :].astype(F32)).astype(BF16)


def back_kernel(jobs, values, panel, w, x1, x2, x3, y1, x0, y0, vals, gs, acc, sem):
    s, _, _ = position()
    per, tile = values.shape[0] // N, values.shape[1]
    pieces = gs.shape[1] // tile
    half = pieces // 2
    copies = [pltpu.make_async_copy(panel, gs, sem.at[N])]
    for k in ORDER:
        rows = pl.ds(target(s, k) * per, per)
        copies.append(pltpu.make_async_copy(values.at[rows], vals.at[rows], sem.at[k]))
    for copy in copies:
        copy.start()
    acc[...] = jnp.zeros_like(acc)
    vals[N * per] = jnp.zeros(vals.shape[1:], vals.dtype)
    xs = (x0, x1, x2, x3)
    for out in xs[1:]:
        out[2 * half * tile :, :] = w[...].astype(BF16)
    for high in range(2):
        for copy in copies[5:] if high else copies[:5]:
            copy.wait()
        base = high * (4 * pieces + 1)

        def rows_of(g):
            return gs[g // pieces, pl.ds(pl.multiple_of((g % pieces) * tile, tile), tile), :]

        def body(q, ta, ga, tb, gb):
            both = jnp.concatenate([vals[ta], vals[tb]], axis=0)
            blocks = jnp.concatenate([rows_of(ga), rows_of(gb)], axis=0)
            acc[base + q] += lax.dot_general(both, blocks, (((0,), (0,)), ((), ())), preferred_element_type=F32)

        run_pairs(high, jobs, body)
        y = (y0, y1)[high]
        for b in range(4):
            for p in range(half):
                out, row = xs[b], (high * half + p) * tile
                out[row : row + tile, :] = acc[base + b * pieces + p].astype(out.dtype)
                row = (b * half + p) * tile
                y[row : row + tile, :] = acc[base + b * pieces + half + p].astype(y.dtype)


def middle_kernel(w, x0, y0, x1, x2, x3, y1, message, z1, z2, z3, top, low):
    rows = top.shape[0]
    message[rows : rows + w.shape[0], :] = w[...].astype(BF16)
    for b, x in enumerate((x1, x2, x3), 1):
        at = rows + b * w.shape[0]
        message[at : at + w.shape[0], :] = x[2 * rows :, :]
    sums = x0[...]
    for x in (x1, x2, x3):
        sums = sums + x[: 2 * rows, :].astype(F32)
    top[...] = sums[:rows, :]
    message[:rows, :] = sums[rows:, :].astype(BF16)
    for b, z in enumerate((low, z1, z2, z3)):
        at = slice(b * rows, (b + 1) * rows)
        z[...] = (y0[at, :] + y1[at, :].astype(F32)).astype(z.dtype)


def dense_kernel(*refs):
    parts, (cot, weight), (act, agg_grad, term) = refs[:N], refs[N : N + 2], refs[N + 2 :]
    agg = parts[0][...].astype(F32)
    for part in parts[1:]:
        agg = agg + part[...].astype(F32)
    low = agg.astype(BF16)
    pre = jnp.dot(low, weight[...], preferred_element_type=F32)
    root = 0.7978845608028654
    square = pre * pre
    t = jnp.tanh(root * pre * (1.0 + 0.044715 * square))
    act[...] = (0.5 * pre * (1.0 + t)).astype(BF16)
    slope = 0.5 * (1.0 + t) + 0.5 * pre * (1.0 - t * t) * (root * (1.0 + 3.0 * 0.044715 * square))
    pre_grad = (cot[...].astype(F32) * slope).astype(BF16)
    term[...] = lax.dot_general(low, pre_grad, (((0,), (0,)), ((), ())), preferred_element_type=F32)
    agg_grad[...] = lax.dot_general(
        pre_grad, weight[...], (((1,), (1,)), ((), ())), preferred_element_type=F32
    ).astype(BF16)


def finish_kernel(order, own, got, top, low, z1, z2, z3, out, grad):
    s, _, _ = position()
    rows = top.shape[0]
    part = grad.shape[0] // N
    for high, message in enumerate((own, got)):
        for b in range(4):
            at = pl.multiple_of(source(s, high * 4 + b) * part, part)
            grad[pl.ds(at, part), :] = message[rows + b * part : rows + (b + 1) * part, :].astype(F32)
    upper = (top[...] + got[:rows, :].astype(F32)).astype(BF16)
    lower = low[...]
    for z in (z1, z2, z3):
        lower = lower + z[...].astype(F32)
    total = jnp.concatenate([upper, lower.astype(BF16)], axis=0)
    blk = total.shape[0]
    place = lax.broadcasted_iota(jnp.int32, (blk, blk), 0) == order[...]
    out[...] = jnp.dot(place.astype(BF16), total, preferred_element_type=F32).astype(BF16)


def reorder_kernel(order, features, out):
    blk = features.shape[0]
    pick = lax.broadcasted_iota(jnp.int32, (blk, blk), 0) == order[...]
    out[...] = lax.dot_general(
        pick.astype(BF16), features[...], (((0,), (0,)), ((), ())), preferred_element_type=F32
    ).astype(BF16)


VMEM = pl.BlockSpec(memory_space=pltpu.VMEM)
SMEM = pl.BlockSpec(memory_space=pltpu.SMEM)
HBM = pl.BlockSpec(memory_space=pltpu.HBM)
MIB = 1 << 20


def shards(features, order, tile_rows, tile_cols, tile_live, tile_values, weight, cotangent):
    blk, width = features.shape
    tile = tile_values.shape[-1]
    pieces = blk // tile
    half = blk // 2
    values = tile_values[0, 0]
    s = lax.axis_index("section")
    d = lax.axis_index("dom")
    c, core = d >> 1, d & 1
    block = jax.ShapeDtypeStruct((blk, width), BF16)
    held = pltpu.VMEM((blk, width), BF16)
    stack = pltpu.VMEM((2 * N * pieces + 1, tile, width), F32)
    params = pltpu.CompilerParams(vmem_limit_bytes=24 * MIB)

    def together(*arrays):
        return lax.optimization_barrier(arrays)

    reordered = pl.pallas_call(
        reorder_kernel, out_shape=held, in_specs=[VMEM] * 2, out_specs=VMEM, name="reorder"
    )(order, features)
    first = {k: to_section(reordered, k) if k else reordered for k in NEAR}
    tiles = (tile_live[0, 0] << 16) | (tile_rows[0, 0] << 8) | tile_cols[0, 0]
    stored = values
    values, acc, jobs, own = pl.pallas_call(
        prepare_kernel,
        out_shape=[
            pltpu.VMEM(stored.shape, BF16),
            stack,
            jax.ShapeDtypeStruct((2 * LIST + 2,), jnp.int32),
            held,
        ],
        in_specs=[SMEM, HBM, VMEM],
        out_specs=[VMEM] * 2 + [SMEM, VMEM],
        scratch_shapes=[pltpu.SemaphoreType.DMA((2,))],
        compiler_params=pltpu.CompilerParams(vmem_limit_bytes=44 * MIB),
        name="prepare",
    )(tiles, stored, reordered)
    first[4], acc = together(first[4], acc)
    second = {k: to_section(first[4], k & 3) for k in FAR}
    flops = 96 * tile * tile * width * 2
    cost = pl.CostEstimate(flops=flops, bytes_accessed=12 * MIB, transcendentals=0)
    acc = pl.pallas_call(
        near_kernel,
        out_shape=stack,
        in_specs=[SMEM] + [VMEM] * (len(NEAR) + 2),
        out_specs=VMEM,
        scratch_shapes=[pltpu.VMEM((len(NEAR), blk, width), BF16), pltpu.SemaphoreType.DMA((len(NEAR),))],
        input_output_aliases={2: 0},
        compiler_params=params,
        cost_estimate=cost,
        name="aggregate_near",
    )(jobs, values, acc, *[first[k] if k else own for k in NEAR])
    four = pltpu.VMEM((N // 2, blk, width), BF16)
    acc, across, along = pl.pallas_call(
        far_kernel,
        out_shape=[stack, four, four],
        in_specs=[SMEM] + [VMEM] * (len(FAR) + 2),
        out_specs=[VMEM] * 3,
        scratch_shapes=[pltpu.VMEM((len(FAR), blk, width), BF16), pltpu.SemaphoreType.DMA((len(FAR),))],
        input_output_aliases={2: 0},
        compiler_params=params,
        cost_estimate=cost,
        name="aggregate_far",
    )(jobs, values, acc, *[second[k] for k in FAR])

    def pair_sums(start, other):
        return pl.pallas_call(
            functools.partial(pair_kernel, start),
            out_shape=[held] * (N // 2),
            in_specs=[VMEM] * 2,
            out_specs=[VMEM] * (N // 2),
            compiler_params=params,
            name=f"pair_{start}",
        )(acc, other)

    across, along = to_core(across), to_core(along)
    far_sums = pair_sums(N // 2, across)
    near_sums = pair_sums(0, along)
    sums = [*near_sums, *far_sums]
    arrived = [to_chip(sums[k], k) if k else sums[k] for k in (1, 3, 6, 5, 7, 4, 2, 0)]

    activated, agg_grad, term = pl.pallas_call(
        dense_kernel,
        out_shape=[block, block, pltpu.VMEM((width, width), F32)],
        in_specs=[VMEM] * (N + 2),
        out_specs=[VMEM] * 3,
        compiler_params=params,
        name="dense",
    )(*arrived, cotangent, weight)

    def swap(x, axis, bit):
        n = lax.axis_size(axis)
        return lax.ppermute(x, axis, [(i, i ^ bit) for i in range(n)])

    def halve(x, bit):
        n = x.shape[0] // 2
        high = (s & bit) != 0
        keep = jnp.where(high, x[n:], x[:n])
        return keep + swap(jnp.where(high, x[:n], x[n:]), "section", bit)

    panel = lax.all_gather(agg_grad, "dom", axis=0)
    w = halve(halve(term, 4), 2)
    jobs = pl.pallas_call(
        functools.partial(prepare_back_kernel, pieces),
        out_shape=jax.ShapeDtypeStruct((2 * LIST + 2,), jnp.int32),
        in_specs=[SMEM, VMEM],
        out_specs=SMEM,
        scratch_shapes=[pltpu.SMEM((stored.shape[0] * pieces,), jnp.int32), pltpu.SMEM((N * pieces,), jnp.int32)],
        name="prepare_back",
    )(tiles, w)
    w = halve(w, 1)
    jobs, w = together(jobs, w)
    for bit in (8, 4, 2, 1):
        w = w + swap(w, "dom", bit)
    panel, w = together(panel, w)
    part = w.shape[0]

    def wide(rows, dtype=BF16):
        return pltpu.VMEM((rows, width), dtype)

    x1, x2, x3, y1, x0, y0 = pl.pallas_call(
        back_kernel,
        out_shape=[wide(blk + part)] * 3 + [wide(2 * blk), wide(blk, F32), wide(2 * blk, F32)],
        in_specs=[SMEM] + [HBM] * 2 + [VMEM],
        out_specs=[VMEM] * 6,
        scratch_shapes=[
            pltpu.VMEM((stored.shape[0] + 1, tile, tile), BF16),
            pltpu.VMEM(panel.shape, BF16),
            pltpu.VMEM((N * pieces + 2, tile, width), F32),
            pltpu.SemaphoreType.DMA((N + 1,)),
        ],
        compiler_params=pltpu.CompilerParams(vmem_limit_bytes=56 * MIB),
        cost_estimate=cost,
        name="aggregate_back",
    )(jobs, stored, panel, w)
    message, z1, z2, z3, top, low = pl.pallas_call(
        middle_kernel,
        out_shape=[wide(half + 4 * part)] + [wide(half)] * 3 + [wide(half, F32)] * 2,
        in_specs=[VMEM] * 7,
        out_specs=[VMEM] * 6,
        compiler_params=params,
        name="middle",
    )(w, x0, y0, to_section(x1, 1), to_section(x2, 2), to_section(x3, 3), to_section(y1, 4))
    feature_grad, weight_grad = pl.pallas_call(
        finish_kernel,
        out_shape=[block, jax.ShapeDtypeStruct((width, width), F32)],
        in_specs=[VMEM] * 8,
        out_specs=[VMEM] * 2,
        compiler_params=params,
        name="finish",
    )(
        order, message, to_section(message, 4), top, low, to_section(z1, 1), to_section(z2, 2), to_section(z3, 3)
    )
    return (activated, feature_grad, weight_grad)


def solution(mesh):
    return jax.shard_map(
        shards,
        mesh=mesh,
        in_specs=(
            P(("section", "dom"), None),
            P(("section", "dom"), None),
            P("section", "dom", None),
            P("section", "dom", None),
            P("section", "dom", None),
            P("section", "dom", None, None, None),
            P(),
            P(("section", "dom"), None),
        ),
        out_specs=(P(("section", "dom"), None), P(("section", "dom"), None), P()),
        check_vma=False,
    )
```

```python
import functools

import jax
import jax.numpy as jnp
from jax import lax
from jax.experimental import pallas as pl
from jax.experimental.pallas import tpu as pltpu
from jax.sharding import PartitionSpec as P

F32 = jnp.float32
BF16 = jnp.bfloat16
N = 8
GROUP = 24
PAIRS = 16
LIST = 144
NEAR, FAR = (4, 1, 3, 2, 0), (5, 7, 6)
ORDER = tuple(range(N))


def target(i, k):
    return ((i >> 2) ^ (k >> 2)) * 4 + ((i + k) & 3)


def source(i, k):
    return ((i >> 2) ^ (k >> 2)) * 4 + ((i - k) & 3)


def offset(i, j):
    return ((i >> 2) ^ (j >> 2)) * 4 + ((i - j) & 3)


def to_section(x, k):
    return lax.ppermute(x, "section", [(i, target(i, k)) for i in range(N)])


def to_chip(x, k):
    return lax.ppermute(x, "dom", [(2 * i + q, 2 * target(i, k) + q) for i in range(N) for q in range(2)])


def to_core(x):
    return lax.ppermute(x, "dom", [(d, d ^ 1) for d in range(2 * N)])


def position():
    d = lax.axis_index("dom")
    return lax.axis_index("section"), d >> 1, d & 1


def look(k, lists):
    which, rank = jnp.int32(0), jnp.int32(0)
    for n, slots in enumerate(lists):
        for m, slot in enumerate(slots):
            which, rank = jnp.where(k == slot, n, which), jnp.where(k == slot, m, rank)
    return which, rank


def list_tiles(tiles, jobs, lists, where, pieces, spare):
    per = tiles.shape[0] // N
    for n in range(2):
        jobs[2 * LIST + n] = 0

    @pl.loop(0, N)
    def _(j):
        a, rank = look(where(j), lists)
        base = a * LIST

        def one(i, n):
            word = tiles[j * per + i]
            jobs[base + n] = ((j * per + i) << 16) | (word & 0xFF00) | (rank * pieces + (word & 255))
            return n + (word >> 16)

        jobs[2 * LIST + a] = lax.fori_loop(0, per, one, jobs[2 * LIST + a], unroll=True)

    for n in range(len(lists)):
        for i in range(GROUP):
            jobs[n * LIST + jobs[2 * LIST + n] + i] = spare


def prepare_kernel(tiles, values, block, kept, acc, jobs, own, sem):
    copies = [pltpu.make_async_copy(values, kept, sem.at[0]), pltpu.make_async_copy(block, own, sem.at[1])]
    for copy in copies:
        copy.start()
    acc[...] = jnp.zeros_like(acc)
    s, _, _ = position()
    total = acc.shape[0] - 1
    lists = (NEAR, FAR)
    list_tiles(tiles, jobs, lists, lambda j: offset(s, j), total // (2 * N), total << 8)
    for copy in copies:
        copy.wait()


def prepare_back_kernel(pieces, tiles, after, jobs, groups, lengths):
    del after
    s, _, _ = position()
    per = tiles.shape[0] // N
    zero = tiles.shape[0] << 16
    sums = N * pieces
    for q in range(sums):
        lengths[q] = 0

    @pl.loop(0, N)
    def _(j):
        k = offset(j, s)

        def one(i, carry):
            word = tiles[j * per + i]
            col = word & 255
            q = k * pieces + col
            n = lengths[q]
            groups[q * per + n] = ((j * per + i) << 16) | (word & 0xFF00) | (q % (sums // 2))
            lengths[q] = n + (word >> 16)
            return carry

        lax.fori_loop(0, per, one, 0, unroll=True)

    for high in range(2):

        def group(q, done):
            n = lengths[q]

            @pl.when(n & 1 == 1)
            def _():
                groups[q * per + n] = zero

            def pair(i, carry):
                for u in range(2):
                    jobs[high * LIST + 2 * (done + i) + u] = groups[q * per + 2 * i + u]
                return carry

            count = (n + 1) >> 1
            lax.fori_loop(0, count, pair, 0)
            return done + count

        done = lax.fori_loop(high * (sums // 2), (high + 1) * (sums // 2), group, jnp.int32(0))
        jobs[2 * LIST + high] = done
        for i in range(2 * PAIRS):
            jobs[high * LIST + 2 * done + i] = zero | (sums // 2)


def run_pairs(which, jobs, body):
    @pl.loop(0, (jobs[2 * LIST + which] + PAIRS - 1) // PAIRS)
    def _(i):
        for u in range(PAIRS):
            at = which * LIST + 2 * (i * PAIRS + u)
            a, b = jobs[at], jobs[at + 1]
            body(a & 255, a >> 16, (a >> 8) & 255, b >> 16, (b >> 8) & 255)


def run_jobs(which, jobs, body):
    @pl.loop(0, (jobs[2 * LIST + which] + GROUP - 1) // GROUP)
    def _(i):
        for u in range(GROUP):
            job = jobs[which * LIST + i * GROUP + u]
            body(job >> 16, (job >> 8) & 255, job & 255)


def place(blocks, buffer, sem):
    copies = [pltpu.make_async_copy(ref, buffer.at[n], sem.at[n]) for n, ref in enumerate(blocks)]
    for copy in copies:
        copy.start()
    for copy in copies:
        copy.wait()


def near_kernel(jobs, values, before, *refs):
    del before
    blocks, (acc, xs, sem) = refs[:-3], refs[-3:]
    place(blocks, xs, sem)
    multiply(0, jobs, values, xs, acc)


def multiply(which, jobs, values, xs, acc):
    tile = values.shape[1]
    pieces = xs.shape[1] // tile

    def body(t, r, x):
        block = xs[x // pieces, pl.ds(pl.multiple_of((x % pieces) * tile, tile), tile), :]
        acc[r] += jnp.dot(values[t], block, preferred_element_type=F32)

    run_jobs(which, jobs, body)


def far_kernel(jobs, values, before, *refs):
    del before
    blocks, (acc, across, along, xs, sem) = refs[:-5], refs[-5:]
    place(blocks, xs, sem)
    multiply(1, jobs, values, xs, acc)
    tile = values.shape[1]
    pieces = xs.shape[1] // tile
    _, c, core = position()
    for k in range(N):
        first = (target(c, k) * 2 + 1 - core) * pieces
        theirs = across if k >= N // 2 else along
        for p in range(pieces):
            theirs[k % (N // 2), p * tile : (p + 1) * tile, :] = acc[first + p].astype(BF16)


def pair_kernel(start, acc, other, *outs):
    tile = acc.shape[1]
    pieces = other.shape[1] // tile
    _, c, core = position()
    for n, out in enumerate(outs):
        k = start + n
        first = (target(c, k) * 2 + core) * pieces
        for p in range(pieces):
            rows = slice(p * tile, (p + 1) * tile)
            out[rows, :] = (acc[first + p] + other[n, rows, :].astype(F32)).astype(BF16)


def back_kernel(jobs, values, panel, w, x1, x2, x3, y1, x0, y0, vals, gs, acc, sem):
    s, _, _ = position()
    per, tile = values.shape[0] // N, values.shape[1]
    pieces = gs.shape[1] // tile
    half = pieces // 2
    copies = [pltpu.make_async_copy(panel, gs, sem.at[N])]
    for k in ORDER:
        rows = pl.ds(target(s, k) * per, per)
        copies.append(pltpu.make_async_copy(values.at[rows], vals.at[rows], sem.at[k]))
    for copy in copies:
        copy.start()
    acc[...] = jnp.zeros_like(acc)
    vals[N * per] = jnp.zeros(vals.shape[1:], vals.dtype)
    xs = (x0, x1, x2, x3)
    for out in xs[1:]:
        out[2 * half * tile :, :] = w[...].astype(BF16)
    for high in range(2):
        for copy in copies[5:] if high else copies[:5]:
            copy.wait()
        base = high * (4 * pieces + 1)

        def rows_of(g):
            return gs[g // pieces, pl.ds(pl.multiple_of((g % pieces) * tile, tile), tile), :]

        def body(q, ta, ga, tb, gb):
            both = jnp.concatenate([vals[ta], vals[tb]], axis=0)
            blocks = jnp.concatenate([rows_of(ga), rows_of(gb)], axis=0)
            acc[base + q] += lax.dot_general(both, blocks, (((0,), (0,)), ((), ())), preferred_element_type=F32)

        run_pairs(high, jobs, body)
        y = (y0, y1)[high]
        for b in range(4):
            for p in range(half):
                out, row = xs[b], (high * half + p) * tile
                out[row : row + tile, :] = acc[base + b * pieces + p].astype(out.dtype)
                row = (b * half + p) * tile
                y[row : row + tile, :] = acc[base + b * pieces + half + p].astype(y.dtype)


def middle_kernel(w, x0, y0, x1, x2, x3, y1, message, z1, z2, z3, top, low):
    rows = top.shape[0]
    message[rows : rows + w.shape[0], :] = w[...].astype(BF16)
    for b, x in enumerate((x1, x2, x3), 1):
        at = rows + b * w.shape[0]
        message[at : at + w.shape[0], :] = x[2 * rows :, :]
    sums = x0[...]
    for x in (x1, x2, x3):
        sums = sums + x[: 2 * rows, :].astype(F32)
    top[...] = sums[:rows, :]
    message[:rows, :] = sums[rows:, :].astype(BF16)
    for b, z in enumerate((low, z1, z2, z3)):
        at = slice(b * rows, (b + 1) * rows)
        z[...] = (y0[at, :] + y1[at, :].astype(F32)).astype(z.dtype)


def dense_kernel(*refs):
    parts, (cot, weight), (act, agg_grad, term) = refs[:N], refs[N : N + 2], refs[N + 2 :]
    agg = parts[0][...].astype(F32)
    for part in parts[1:]:
        agg = agg + part[...].astype(F32)
    low = agg.astype(BF16)
    pre = jnp.dot(low, weight[...], preferred_element_type=F32)
    root = 0.7978845608028654
    square = pre * pre
    t = jnp.tanh(root * pre * (1.0 + 0.044715 * square))
    act[...] = (0.5 * pre * (1.0 + t)).astype(BF16)
    slope = 0.5 * (1.0 + t) + 0.5 * pre * (1.0 - t * t) * (root * (1.0 + 3.0 * 0.044715 * square))
    pre_grad = (cot[...].astype(F32) * slope).astype(BF16)
    term[...] = lax.dot_general(low, pre_grad, (((0,), (0,)), ((), ())), preferred_element_type=F32)
    agg_grad[...] = lax.dot_general(
        pre_grad, weight[...], (((1,), (1,)), ((), ())), preferred_element_type=F32
    ).astype(BF16)


def finish_kernel(order, own, got, top, low, z1, z2, z3, out, grad):
    s, _, _ = position()
    rows = top.shape[0]
    part = grad.shape[0] // N
    for high, message in enumerate((own, got)):
        for b in range(4):
            at = pl.multiple_of(source(s, high * 4 + b) * part, part)
            grad[pl.ds(at, part), :] = message[rows + b * part : rows + (b + 1) * part, :].astype(F32)
    upper = (top[...] + got[:rows, :].astype(F32)).astype(BF16)
    lower = low[...]
    for z in (z1, z2, z3):
        lower = lower + z[...].astype(F32)
    total = jnp.concatenate([upper, lower.astype(BF16)], axis=0)
    blk = total.shape[0]
    place = lax.broadcasted_iota(jnp.int32, (blk, blk), 0) == order[...]
    out[...] = jnp.dot(place.astype(BF16), total, preferred_element_type=F32).astype(BF16)


def reorder_kernel(order, features, out):
    blk = features.shape[0]
    pick = lax.broadcasted_iota(jnp.int32, (blk, blk), 0) == order[...]
    out[...] = lax.dot_general(
        pick.astype(BF16), features[...], (((0,), (0,)), ((), ())), preferred_element_type=F32
    ).astype(BF16)


VMEM = pl.BlockSpec(memory_space=pltpu.VMEM)
SMEM = pl.BlockSpec(memory_space=pltpu.SMEM)
HBM = pl.BlockSpec(memory_space=pltpu.HBM)
MIB = 1 << 20


def shards(features, order, tile_rows, tile_cols, tile_live, tile_values, weight, cotangent):
    blk, width = features.shape
    tile = tile_values.shape[-1]
    pieces = blk // tile
    half = blk // 2
    values = tile_values[0, 0]
    s = lax.axis_index("section")
    d = lax.axis_index("dom")
    c, core = d >> 1, d & 1
    block = jax.ShapeDtypeStruct((blk, width), BF16)
    held = pltpu.VMEM((blk, width), BF16)
    stack = pltpu.VMEM((2 * N * pieces + 1, tile, width), F32)
    params = pltpu.CompilerParams(vmem_limit_bytes=24 * MIB)

    def together(*arrays):
        return lax.optimization_barrier(arrays)

    reordered = pl.pallas_call(
        reorder_kernel, out_shape=held, in_specs=[VMEM] * 2, out_specs=VMEM, name="reorder"
    )(order, features)
    first = {k: to_section(reordered, k) if k else reordered for k in NEAR}
    tiles = (tile_live[0, 0] << 16) | (tile_rows[0, 0] << 8) | tile_cols[0, 0]
    stored = values
    values, acc, jobs, own = pl.pallas_call(
        prepare_kernel,
        out_shape=[
            pltpu.VMEM(stored.shape, BF16),
            stack,
            jax.ShapeDtypeStruct((2 * LIST + 2,), jnp.int32),
            held,
        ],
        in_specs=[SMEM, HBM, VMEM],
        out_specs=[VMEM] * 2 + [SMEM, VMEM],
        scratch_shapes=[pltpu.SemaphoreType.DMA((2,))],
        compiler_params=pltpu.CompilerParams(vmem_limit_bytes=44 * MIB),
        name="prepare",
    )(tiles, stored, reordered)
    first[4], acc = together(first[4], acc)
    second = {k: to_section(first[4], k & 3) for k in FAR}
    flops = 96 * tile * tile * width * 2
    cost = pl.CostEstimate(flops=flops, bytes_accessed=12 * MIB, transcendentals=0)
    acc = pl.pallas_call(
        near_kernel,
        out_shape=stack,
        in_specs=[SMEM] + [VMEM] * (len(NEAR) + 2),
        out_specs=VMEM,
        scratch_shapes=[pltpu.VMEM((len(NEAR), blk, width), BF16), pltpu.SemaphoreType.DMA((len(NEAR),))],
        input_output_aliases={2: 0},
        compiler_params=params,
        cost_estimate=cost,
        name="aggregate_near",
    )(jobs, values, acc, *[first[k] if k else own for k in NEAR])
    four = pltpu.VMEM((N // 2, blk, width), BF16)
    acc, across, along = pl.pallas_call(
        far_kernel,
        out_shape=[stack, four, four],
        in_specs=[SMEM] + [VMEM] * (len(FAR) + 2),
        out_specs=[VMEM] * 3,
        scratch_shapes=[pltpu.VMEM((len(FAR), blk, width), BF16), pltpu.SemaphoreType.DMA((len(FAR),))],
        input_output_aliases={2: 0},
        compiler_params=params,
        cost_estimate=cost,
        name="aggregate_far",
    )(jobs, values, acc, *[second[k] for k in FAR])

    def pair_sums(start, other):
        return pl.pallas_call(
            functools.partial(pair_kernel, start),
            out_shape=[held] * (N // 2),
            in_specs=[VMEM] * 2,
            out_specs=[VMEM] * (N // 2),
            compiler_params=params,
            name=f"pair_{start}",
        )(acc, other)

    across, along = to_core(across), to_core(along)
    far_sums = pair_sums(N // 2, across)
    near_sums = pair_sums(0, along)
    sums = [*near_sums, *far_sums]
    arrived = [to_chip(sums[k], k) if k else sums[k] for k in (1, 3, 6, 5, 7, 4, 2, 0)]

    activated, agg_grad, term = pl.pallas_call(
        dense_kernel,
        out_shape=[block, block, pltpu.VMEM((width, width), F32)],
        in_specs=[VMEM] * (N + 2),
        out_specs=[VMEM] * 3,
        compiler_params=params,
        name="dense",
    )(*arrived, cotangent, weight)

    def swap(x, axis, bit):
        n = lax.axis_size(axis)
        return lax.ppermute(x, axis, [(i, i ^ bit) for i in range(n)])

    def halve(x, bit):
        n = x.shape[0] // 2
        high = (s & bit) != 0
        keep = jnp.where(high, x[n:], x[:n])
        return keep + swap(jnp.where(high, x[:n], x[n:]), "section", bit)

    panel = lax.all_gather(agg_grad, "dom", axis=0)
    w = halve(halve(term, 4), 2)
    jobs = pl.pallas_call(
        functools.partial(prepare_back_kernel, pieces),
        out_shape=jax.ShapeDtypeStruct((2 * LIST + 2,), jnp.int32),
        in_specs=[SMEM, VMEM],
        out_specs=SMEM,
        scratch_shapes=[pltpu.SMEM((stored.shape[0] * pieces,), jnp.int32), pltpu.SMEM((N * pieces,), jnp.int32)],
        name="prepare_back",
    )(tiles, w)
    w = halve(w, 1)
    jobs, w = together(jobs, w)
    for bit in (8, 4, 2, 1):
        w = w + swap(w, "dom", bit)
    panel, w = together(panel, w)
    part = w.shape[0]

    def wide(rows, dtype=BF16):
        return pltpu.VMEM((rows, width), dtype)

    x1, x2, x3, y1, x0, y0 = pl.pallas_call(
        back_kernel,
        out_shape=[wide(blk + part)] * 3 + [wide(2 * blk), wide(blk, F32), wide(2 * blk, F32)],
        in_specs=[SMEM] + [HBM] * 2 + [VMEM],
        out_specs=[VMEM] * 6,
        scratch_shapes=[
            pltpu.VMEM((stored.shape[0] + 1, tile, tile), BF16),
            pltpu.VMEM(panel.shape, BF16),
            pltpu.VMEM((N * pieces + 2, tile, width), F32),
            pltpu.SemaphoreType.DMA((N + 1,)),
        ],
        compiler_params=pltpu.CompilerParams(vmem_limit_bytes=56 * MIB),
        cost_estimate=cost,
        name="aggregate_back",
    )(jobs, stored, panel, w)
    message, z1, z2, z3, top, low = pl.pallas_call(
        middle_kernel,
        out_shape=[wide(half + 4 * part)] + [wide(half)] * 3 + [wide(half, F32)] * 2,
        in_specs=[VMEM] * 7,
        out_specs=[VMEM] * 6,
        compiler_params=params,
        name="middle",
    )(w, x0, y0, to_section(x1, 1), to_section(x2, 2), to_section(x3, 3), to_section(y1, 4))
    feature_grad, weight_grad = pl.pallas_call(
        finish_kernel,
        out_shape=[block, jax.ShapeDtypeStruct((width, width), F32)],
        in_specs=[VMEM] * 8,
        out_specs=[VMEM] * 2,
        compiler_params=params,
        name="finish",
    )(
        order, message, to_section(message, 4), top, low, to_section(z1, 1), to_section(z2, 2), to_section(z3, 3)
    )
    return (activated, feature_grad, weight_grad)


def solution(mesh):
    return jax.shard_map(
        shards,
        mesh=mesh,
        in_specs=(
            P(("section", "dom"), None),
            P(("section", "dom"), None),
            P("section", "dom", None),
            P("section", "dom", None),
            P("section", "dom", None),
            P("section", "dom", None, None, None),
            P(),
            P(("section", "dom"), None),
        ),
        out_specs=(P(("section", "dom"), None), P(("section", "dom"), None), P()),
        check_vma=False,
    )
```

```python
import functools

import jax
import jax.numpy as jnp
from jax import lax
from jax.experimental import pallas as pl
from jax.experimental.pallas import tpu as pltpu
from jax.sharding import PartitionSpec as P

F32 = jnp.float32
BF16 = jnp.bfloat16
N = 8
GROUP = 24
PAIRS = 16
LIST = 144
NEAR, FAR = (2, 4, 1, 3, 0), (5, 7, 6)
ORDER = tuple(range(N))


def target(i, k):
    return ((i >> 2) ^ (k >> 2)) * 4 + ((i + k) & 3)


def source(i, k):
    return ((i >> 2) ^ (k >> 2)) * 4 + ((i - k) & 3)


def offset(i, j):
    return ((i >> 2) ^ (j >> 2)) * 4 + ((i - j) & 3)


def to_section(x, k):
    return lax.ppermute(x, "section", [(i, target(i, k)) for i in range(N)])


def to_chip(x, k):
    return lax.ppermute(x, "dom", [(2 * i + q, 2 * target(i, k) + q) for i in range(N) for q in range(2)])


def to_core(x):
    return lax.ppermute(x, "dom", [(d, d ^ 1) for d in range(2 * N)])


def position():
    d = lax.axis_index("dom")
    return lax.axis_index("section"), d >> 1, d & 1


def look(k, lists):
    which, rank = jnp.int32(0), jnp.int32(0)
    for n, slots in enumerate(lists):
        for m, slot in enumerate(slots):
            which, rank = jnp.where(k == slot, n, which), jnp.where(k == slot, m, rank)
    return which, rank


def list_tiles(tiles, jobs, lists, where, pieces, spare):
    per = tiles.shape[0] // N
    for n in range(2):
        jobs[2 * LIST + n] = 0

    @pl.loop(0, N)
    def _(j):
        a, rank = look(where(j), lists)
        base = a * LIST

        def one(i, n):
            word = tiles[j * per + i]
            jobs[base + n] = ((j * per + i) << 16) | (word & 0xFF00) | (rank * pieces + (word & 255))
            return n + (word >> 16)

        jobs[2 * LIST + a] = lax.fori_loop(0, per, one, jobs[2 * LIST + a], unroll=True)

    for n in range(len(lists)):
        for i in range(GROUP):
            jobs[n * LIST + jobs[2 * LIST + n] + i] = spare


def prepare_kernel(tiles, values, block, kept, acc, jobs, own, sem):
    copies = [pltpu.make_async_copy(values, kept, sem.at[0]), pltpu.make_async_copy(block, own, sem.at[1])]
    for copy in copies:
        copy.start()
    acc[...] = jnp.zeros_like(acc)
    s, _, _ = position()
    total = acc.shape[0] - 1
    lists = (NEAR, FAR)
    list_tiles(tiles, jobs, lists, lambda j: offset(s, j), total // (2 * N), total << 8)
    for copy in copies:
        copy.wait()


def prepare_back_kernel(pieces, tiles, after, jobs, groups, lengths):
    del after
    s, _, _ = position()
    per = tiles.shape[0] // N
    zero = tiles.shape[0] << 16
    sums = N * pieces
    for q in range(sums):
        lengths[q] = 0

    @pl.loop(0, N)
    def _(j):
        k = offset(j, s)

        def one(i, carry):
            word = tiles[j * per + i]
            col = word & 255
            q = k * pieces + col
            n = lengths[q]
            groups[q * per + n] = ((j * per + i) << 16) | (word & 0xFF00) | (q % (sums // 2))
            lengths[q] = n + (word >> 16)
            return carry

        lax.fori_loop(0, per, one, 0, unroll=True)

    for high in range(2):

        def group(q, done):
            n = lengths[q]

            @pl.when(n & 1 == 1)
            def _():
                groups[q * per + n] = zero

            def pair(i, carry):
                for u in range(2):
                    jobs[high * LIST + 2 * (done + i) + u] = groups[q * per + 2 * i + u]
                return carry

            count = (n + 1) >> 1
            lax.fori_loop(0, count, pair, 0)
            return done + count

        done = lax.fori_loop(high * (sums // 2), (high + 1) * (sums // 2), group, jnp.int32(0))
        jobs[2 * LIST + high] = done
        for i in range(2 * PAIRS):
            jobs[high * LIST + 2 * done + i] = zero | (sums // 2)


def run_pairs(which, jobs, body):
    @pl.loop(0, (jobs[2 * LIST + which] + PAIRS - 1) // PAIRS)
    def _(i):
        for u in range(PAIRS):
            at = which * LIST + 2 * (i * PAIRS + u)
            a, b = jobs[at], jobs[at + 1]
            body(a & 255, a >> 16, (a >> 8) & 255, b >> 16, (b >> 8) & 255)


def run_jobs(which, jobs, body):
    @pl.loop(0, (jobs[2 * LIST + which] + GROUP - 1) // GROUP)
    def _(i):
        for u in range(GROUP):
            job = jobs[which * LIST + i * GROUP + u]
            body(job >> 16, (job >> 8) & 255, job & 255)


def place(blocks, buffer, sem):
    copies = [pltpu.make_async_copy(ref, buffer.at[n], sem.at[n]) for n, ref in enumerate(blocks)]
    for copy in copies:
        copy.start()
    for copy in copies:
        copy.wait()


def near_kernel(jobs, values, before, *refs):
    del before
    blocks, (acc, xs, sem) = refs[:-3], refs[-3:]
    place(blocks, xs, sem)
    multiply(0, jobs, values, xs, acc)


def multiply(which, jobs, values, xs, acc):
    tile = values.shape[1]
    pieces = xs.shape[1] // tile

    def body(t, r, x):
        block = xs[x // pieces, pl.ds(pl.multiple_of((x % pieces) * tile, tile), tile), :]
        acc[r] += jnp.dot(values[t], block, preferred_element_type=F32)

    run_jobs(which, jobs, body)


def far_kernel(jobs, values, before, *refs):
    del before
    blocks, (acc, across, along, xs, sem) = refs[:-5], refs[-5:]
    place(blocks, xs, sem)
    multiply(1, jobs, values, xs, acc)
    tile = values.shape[1]
    pieces = xs.shape[1] // tile
    _, c, core = position()
    for k in range(N):
        first = (target(c, k) * 2 + 1 - core) * pieces
        theirs = across if k >= N // 2 else along
        for p in range(pieces):
            theirs[k % (N // 2), p * tile : (p + 1) * tile, :] = acc[first + p].astype(BF16)


def pair_kernel(start, acc, other, *outs):
    tile = acc.shape[1]
    pieces = other.shape[1] // tile
    _, c, core = position()
    for n, out in enumerate(outs):
        k = start + n
        first = (target(c, k) * 2 + core) * pieces
        for p in range(pieces):
            rows = slice(p * tile, (p + 1) * tile)
            out[rows, :] = (acc[first + p] + other[n, rows, :].astype(F32)).astype(BF16)


def back_kernel(jobs, values, panel, w, x1, x2, x3, y1, x0, y0, vals, gs, acc, sem):
    s, _, _ = position()
    per, tile = values.shape[0] // N, values.shape[1]
    pieces = gs.shape[1] // tile
    half = pieces // 2
    copies = [pltpu.make_async_copy(panel, gs, sem.at[N])]
    for k in ORDER:
        rows = pl.ds(target(s, k) * per, per)
        copies.append(pltpu.make_async_copy(values.at[rows], vals.at[rows], sem.at[k]))
    for copy in copies:
        copy.start()
    acc[...] = jnp.zeros_like(acc)
    vals[N * per] = jnp.zeros(vals.shape[1:], vals.dtype)
    xs = (x0, x1, x2, x3)
    for out in xs[1:]:
        out[2 * half * tile :, :] = w[...].astype(BF16)
    for high in range(2):
        for copy in copies[5:] if high else copies[:5]:
            copy.wait()
        base = high * (4 * pieces + 1)

        def rows_of(g):
            return gs[g // pieces, pl.ds(pl.multiple_of((g % pieces) * tile, tile), tile), :]

        def body(q, ta, ga, tb, gb):
            both = jnp.concatenate([vals[ta], vals[tb]], axis=0)
            blocks = jnp.concatenate([rows_of(ga), rows_of(gb)], axis=0)
            acc[base + q] += lax.dot_general(both, blocks, (((0,), (0,)), ((), ())), preferred_element_type=F32)

        run_pairs(high, jobs, body)
        y = (y0, y1)[high]
        for b in range(4):
            for p in range(half):
                out, row = xs[b], (high * half + p) * tile
                out[row : row + tile, :] = acc[base + b * pieces + p].astype(out.dtype)
                row = (b * half + p) * tile
                y[row : row + tile, :] = acc[base + b * pieces + half + p].astype(y.dtype)


def middle_kernel(w, x0, y0, y1, x1, x3, x2, message, z1, z2, z3, top, low):
    rows = top.shape[0]
    message[rows : rows + w.shape[0], :] = w[...].astype(BF16)
    for b, x in enumerate((x1, x2, x3), 1):
        at = rows + b * w.shape[0]
        message[at : at + w.shape[0], :] = x[2 * rows :, :]
    sums = x0[...]
    for x in (x1, x2, x3):
        sums = sums + x[: 2 * rows, :].astype(F32)
    top[...] = sums[:rows, :]
    message[:rows, :] = sums[rows:, :].astype(BF16)
    for b, z in enumerate((low, z1, z2, z3)):
        at = slice(b * rows, (b + 1) * rows)
        z[...] = (y0[at, :] + y1[at, :].astype(F32)).astype(z.dtype)


def dense_kernel(*refs):
    parts, (cot, weight), (act, agg_grad, term) = refs[:N], refs[N : N + 2], refs[N + 2 :]
    agg = parts[0][...].astype(F32)
    for part in parts[1:]:
        agg = agg + part[...].astype(F32)
    low = agg.astype(BF16)
    pre = jnp.dot(low, weight[...], preferred_element_type=F32)
    root = 0.7978845608028654
    square = pre * pre
    t = jnp.tanh(root * pre * (1.0 + 0.044715 * square))
    act[...] = (0.5 * pre * (1.0 + t)).astype(BF16)
    slope = 0.5 * (1.0 + t) + 0.5 * pre * (1.0 - t * t) * (root * (1.0 + 3.0 * 0.044715 * square))
    pre_grad = (cot[...].astype(F32) * slope).astype(BF16)
    term[...] = lax.dot_general(low, pre_grad, (((0,), (0,)), ((), ())), preferred_element_type=F32)
    agg_grad[...] = lax.dot_general(
        pre_grad, weight[...], (((1,), (1,)), ((), ())), preferred_element_type=F32
    ).astype(BF16)


def finish_kernel(order, own, got, top, low, z1, z2, z3, out, grad):
    s, _, _ = position()
    rows = top.shape[0]
    part = grad.shape[0] // N
    for high, message in enumerate((own, got)):
        for b in range(4):
            at = pl.multiple_of(source(s, high * 4 + b) * part, part)
            grad[pl.ds(at, part), :] = message[rows + b * part : rows + (b + 1) * part, :].astype(F32)
    upper = (top[...] + got[:rows, :].astype(F32)).astype(BF16)
    lower = low[...]
    for z in (z1, z2, z3):
        lower = lower + z[...].astype(F32)
    total = jnp.concatenate([upper, lower.astype(BF16)], axis=0)
    blk = total.shape[0]
    place = lax.broadcasted_iota(jnp.int32, (blk, blk), 0) == order[...]
    out[...] = jnp.dot(place.astype(BF16), total, preferred_element_type=F32).astype(BF16)


def reorder_kernel(order, features, out):
    blk = features.shape[0]
    pick = lax.broadcasted_iota(jnp.int32, (blk, blk), 0) == order[...]
    out[...] = lax.dot_general(
        pick.astype(BF16), features[...], (((0,), (0,)), ((), ())), preferred_element_type=F32
    ).astype(BF16)


VMEM = pl.BlockSpec(memory_space=pltpu.VMEM)
SMEM = pl.BlockSpec(memory_space=pltpu.SMEM)
HBM = pl.BlockSpec(memory_space=pltpu.HBM)
MIB = 1 << 20


def shards(features, order, tile_rows, tile_cols, tile_live, tile_values, weight, cotangent):
    blk, width = features.shape
    tile = tile_values.shape[-1]
    pieces = blk // tile
    half = blk // 2
    values = tile_values[0, 0]
    s = lax.axis_index("section")
    d = lax.axis_index("dom")
    c, core = d >> 1, d & 1
    block = jax.ShapeDtypeStruct((blk, width), BF16)
    held = pltpu.VMEM((blk, width), BF16)
    stack = pltpu.VMEM((2 * N * pieces + 1, tile, width), F32)
    params = pltpu.CompilerParams(vmem_limit_bytes=24 * MIB)

    def together(*arrays):
        return lax.optimization_barrier(arrays)

    reordered = pl.pallas_call(
        reorder_kernel, out_shape=held, in_specs=[VMEM] * 2, out_specs=VMEM, name="reorder"
    )(order, features)
    first = {k: to_section(reordered, k) if k else reordered for k in NEAR}
    tiles = (tile_live[0, 0] << 16) | (tile_rows[0, 0] << 8) | tile_cols[0, 0]
    stored = values
    values, acc, jobs, own = pl.pallas_call(
        prepare_kernel,
        out_shape=[
            pltpu.VMEM(stored.shape, BF16),
            stack,
            jax.ShapeDtypeStruct((2 * LIST + 2,), jnp.int32),
            held,
        ],
        in_specs=[SMEM, HBM, VMEM],
        out_specs=[VMEM] * 2 + [SMEM, VMEM],
        scratch_shapes=[pltpu.SemaphoreType.DMA((2,))],
        compiler_params=pltpu.CompilerParams(vmem_limit_bytes=44 * MIB),
        name="prepare",
    )(tiles, stored, reordered)
    first[2], first[4], acc = together(first[2], first[4], acc)
    second = {5: to_section(first[4], 1), 7: to_section(first[4], 3), 6: to_section(first[2], 4)}
    flops = 96 * tile * tile * width * 2
    cost = pl.CostEstimate(flops=flops, bytes_accessed=12 * MIB, transcendentals=0)
    acc = pl.pallas_call(
        near_kernel,
        out_shape=stack,
        in_specs=[SMEM] + [VMEM] * (len(NEAR) + 2),
        out_specs=VMEM,
        scratch_shapes=[pltpu.VMEM((len(NEAR), blk, width), BF16), pltpu.SemaphoreType.DMA((len(NEAR),))],
        input_output_aliases={2: 0},
        compiler_params=params,
        cost_estimate=cost,
        name="aggregate_near",
    )(jobs, values, acc, *[first[k] if k else own for k in NEAR])
    four = pltpu.VMEM((N // 2, blk, width), BF16)
    acc, across, along = pl.pallas_call(
        far_kernel,
        out_shape=[stack, four, four],
        in_specs=[SMEM] + [VMEM] * (len(FAR) + 2),
        out_specs=[VMEM] * 3,
        scratch_shapes=[pltpu.VMEM((len(FAR), blk, width), BF16), pltpu.SemaphoreType.DMA((len(FAR),))],
        input_output_aliases={2: 0},
        compiler_params=params,
        cost_estimate=cost,
        name="aggregate_far",
    )(jobs, values, acc, *[second[k] for k in FAR])

    def pair_sums(start, other):
        return pl.pallas_call(
            functools.partial(pair_kernel, start),
            out_shape=[held] * (N // 2),
            in_specs=[VMEM] * 2,
            out_specs=[VMEM] * (N // 2),
            compiler_params=params,
            name=f"pair_{start}",
        )(acc, other)

    across, along = to_core(across), to_core(along)
    far_sums = pair_sums(N // 2, across)
    near_sums = pair_sums(0, along)
    sums = [*near_sums, *far_sums]
    arrived = [to_chip(sums[k], k) if k else sums[k] for k in (1, 3, 6, 5, 7, 4, 2, 0)]

    activated, agg_grad, term = pl.pallas_call(
        dense_kernel,
        out_shape=[block, block, pltpu.VMEM((width, width), F32)],
        in_specs=[VMEM] * (N + 2),
        out_specs=[VMEM] * 3,
        compiler_params=params,
        name="dense",
    )(*arrived, cotangent, weight)

    def swap(x, axis, bit):
        n = lax.axis_size(axis)
        return lax.ppermute(x, axis, [(i, i ^ bit) for i in range(n)])

    def halve(x, bit):
        n = x.shape[0] // 2
        high = (s & bit) != 0
        keep = jnp.where(high, x[n:], x[:n])
        return keep + swap(jnp.where(high, x[:n], x[n:]), "section", bit)

    panel = lax.all_gather(agg_grad, "dom", axis=0)
    w = halve(halve(term, 4), 2)
    jobs = pl.pallas_call(
        functools.partial(prepare_back_kernel, pieces),
        out_shape=jax.ShapeDtypeStruct((2 * LIST + 2,), jnp.int32),
        in_specs=[SMEM, VMEM],
        out_specs=SMEM,
        scratch_shapes=[pltpu.SMEM((stored.shape[0] * pieces,), jnp.int32), pltpu.SMEM((N * pieces,), jnp.int32)],
        name="prepare_back",
    )(tiles, w)
    w = halve(w, 1)
    jobs, w = together(jobs, w)
    for bit in (8, 4, 2, 1):
        w = w + swap(w, "dom", bit)
    panel, w = together(panel, w)
    part = w.shape[0]

    def wide(rows, dtype=BF16):
        return pltpu.VMEM((rows, width), dtype)

    x1, x2, x3, y1, x0, y0 = pl.pallas_call(
        back_kernel,
        out_shape=[wide(blk + part)] * 3 + [wide(2 * blk), wide(blk, F32), wide(2 * blk, F32)],
        in_specs=[SMEM] + [HBM] * 2 + [VMEM],
        out_specs=[VMEM] * 6,
        scratch_shapes=[
            pltpu.VMEM((stored.shape[0] + 1, tile, tile), BF16),
            pltpu.VMEM(panel.shape, BF16),
            pltpu.VMEM((N * pieces + 2, tile, width), F32),
            pltpu.SemaphoreType.DMA((N + 1,)),
        ],
        compiler_params=pltpu.CompilerParams(vmem_limit_bytes=56 * MIB),
        cost_estimate=cost,
        name="aggregate_back",
    )(jobs, stored, panel, w)
    message, z1, z2, z3, top, low = pl.pallas_call(
        middle_kernel,
        out_shape=[wide(half + 4 * part)] + [wide(half)] * 3 + [wide(half, F32)] * 2,
        in_specs=[VMEM] * 7,
        out_specs=[VMEM] * 6,
        compiler_params=params,
        name="middle",
    )(w, x0, y0, to_section(y1, 4), to_section(x1, 1), to_section(x3, 3), to_section(x2, 2))
    feature_grad, weight_grad = pl.pallas_call(
        finish_kernel,
        out_shape=[block, jax.ShapeDtypeStruct((width, width), F32)],
        in_specs=[VMEM] * 8,
        out_specs=[VMEM] * 2,
        compiler_params=params,
        name="finish",
    )(
        order, message, to_section(message, 4), top, low, to_section(z1, 1), to_section(z2, 2), to_section(z3, 3)
    )
    return (activated, feature_grad, weight_grad)


def solution(mesh):
    return jax.shard_map(
        shards,
        mesh=mesh,
        in_specs=(
            P(("section", "dom"), None),
            P(("section", "dom"), None),
            P("section", "dom", None),
            P("section", "dom", None),
            P("section", "dom", None),
            P("section", "dom", None, None, None),
            P(),
            P(("section", "dom"), None),
        ),
        out_specs=(P(("section", "dom"), None), P(("section", "dom"), None), P()),
        check_vma=False,
    )
```

```python
import functools

import jax
import jax.numpy as jnp
from jax import lax
from jax.experimental import pallas as pl
from jax.experimental.pallas import tpu as pltpu
from jax.sharding import PartitionSpec as P

F32 = jnp.float32
BF16 = jnp.bfloat16
N = 8
GROUP = 24
PAIRS = 16
LIST = 144
NEAR, FAR = (2, 1, 4, 3, 0), (5, 7, 6)
ORDER = tuple(range(N))


def target(i, k):
    return ((i >> 2) ^ (k >> 2)) * 4 + ((i + k) & 3)


def source(i, k):
    return ((i >> 2) ^ (k >> 2)) * 4 + ((i - k) & 3)


def offset(i, j):
    return ((i >> 2) ^ (j >> 2)) * 4 + ((i - j) & 3)


def to_section(x, k):
    return lax.ppermute(x, "section", [(i, target(i, k)) for i in range(N)])


def to_chip(x, k):
    return lax.ppermute(x, "dom", [(2 * i + q, 2 * target(i, k) + q) for i in range(N) for q in range(2)])


def to_core(x):
    return lax.ppermute(x, "dom", [(d, d ^ 1) for d in range(2 * N)])


def position():
    d = lax.axis_index("dom")
    return lax.axis_index("section"), d >> 1, d & 1


def look(k, lists):
    which, rank = jnp.int32(0), jnp.int32(0)
    for n, slots in enumerate(lists):
        for m, slot in enumerate(slots):
            which, rank = jnp.where(k == slot, n, which), jnp.where(k == slot, m, rank)
    return which, rank


def list_tiles(tiles, jobs, lists, where, pieces, spare):
    per = tiles.shape[0] // N
    for n in range(2):
        jobs[2 * LIST + n] = 0

    @pl.loop(0, N)
    def _(j):
        a, rank = look(where(j), lists)
        base = a * LIST

        def one(i, n):
            word = tiles[j * per + i]
            jobs[base + n] = ((j * per + i) << 16) | (word & 0xFF00) | (rank * pieces + (word & 255))
            return n + (word >> 16)

        jobs[2 * LIST + a] = lax.fori_loop(0, per, one, jobs[2 * LIST + a], unroll=True)

    for n in range(len(lists)):
        for i in range(GROUP):
            jobs[n * LIST + jobs[2 * LIST + n] + i] = spare


def prepare_kernel(tiles, values, block, kept, acc, jobs, own, sem):
    copies = [pltpu.make_async_copy(values, kept, sem.at[0]), pltpu.make_async_copy(block, own, sem.at[1])]
    for copy in copies:
        copy.start()
    acc[...] = jnp.zeros_like(acc)
    s, _, _ = position()
    total = acc.shape[0] - 1
    lists = (NEAR, FAR)
    list_tiles(tiles, jobs, lists, lambda j: offset(s, j), total // (2 * N), total << 8)
    for copy in copies:
        copy.wait()


def prepare_back_kernel(pieces, tiles, after, jobs, groups, lengths):
    del after
    s, _, _ = position()
    per = tiles.shape[0] // N
    zero = tiles.shape[0] << 16
    sums = N * pieces
    for q in range(sums):
        lengths[q] = 0

    @pl.loop(0, N)
    def _(j):
        k = offset(j, s)

        def one(i, carry):
            word = tiles[j * per + i]
            col = word & 255
            q = k * pieces + col
            n = lengths[q]
            groups[q * per + n] = ((j * per + i) << 16) | (word & 0xFF00) | (q % (sums // 2))
            lengths[q] = n + (word >> 16)
            return carry

        lax.fori_loop(0, per, one, 0, unroll=True)

    for high in range(2):

        def group(q, done):
            n = lengths[q]

            @pl.when(n & 1 == 1)
            def _():
                groups[q * per + n] = zero

            def pair(i, carry):
                for u in range(2):
                    jobs[high * LIST + 2 * (done + i) + u] = groups[q * per + 2 * i + u]
                return carry

            count = (n + 1) >> 1
            lax.fori_loop(0, count, pair, 0)
            return done + count

        done = lax.fori_loop(high * (sums // 2), (high + 1) * (sums // 2), group, jnp.int32(0))
        jobs[2 * LIST + high] = done
        for i in range(2 * PAIRS):
            jobs[high * LIST + 2 * done + i] = zero | (sums // 2)


def run_pairs(which, jobs, body):
    @pl.loop(0, (jobs[2 * LIST + which] + PAIRS - 1) // PAIRS)
    def _(i):
        for u in range(PAIRS):
            at = which * LIST + 2 * (i * PAIRS + u)
            a, b = jobs[at], jobs[at + 1]
            body(a & 255, a >> 16, (a >> 8) & 255, b >> 16, (b >> 8) & 255)


def run_jobs(which, jobs, body):
    @pl.loop(0, (jobs[2 * LIST + which] + GROUP - 1) // GROUP)
    def _(i):
        for u in range(GROUP):
            job = jobs[which * LIST + i * GROUP + u]
            body(job >> 16, (job >> 8) & 255, job & 255)


def place(blocks, buffer, sem):
    copies = [pltpu.make_async_copy(ref, buffer.at[n], sem.at[n]) for n, ref in enumerate(blocks)]
    for copy in copies:
        copy.start()
    for copy in copies:
        copy.wait()


def near_kernel(jobs, values, before, *refs):
    del before
    blocks, (acc, xs, sem) = refs[:-3], refs[-3:]
    place(blocks, xs, sem)
    multiply(0, jobs, values, xs, acc)


def multiply(which, jobs, values, xs, acc):
    tile = values.shape[1]
    pieces = xs.shape[1] // tile

    def body(t, r, x):
        block = xs[x // pieces, pl.ds(pl.multiple_of((x % pieces) * tile, tile), tile), :]
        acc[r] += jnp.dot(values[t], block, preferred_element_type=F32)

    run_jobs(which, jobs, body)


def far_kernel(jobs, values, before, *refs):
    del before
    blocks, (acc, across, along, xs, sem) = refs[:-5], refs[-5:]
    place(blocks, xs, sem)
    multiply(1, jobs, values, xs, acc)
    tile = values.shape[1]
    pieces = xs.shape[1] // tile
    _, c, core = position()
    for k in range(N):
        first = (target(c, k) * 2 + 1 - core) * pieces
        theirs = across if k >= N // 2 else along
        for p in range(pieces):
            theirs[k % (N // 2), p * tile : (p + 1) * tile, :] = acc[first + p].astype(BF16)


def pair_kernel(start, acc, other, *outs):
    tile = acc.shape[1]
    pieces = other.shape[1] // tile
    _, c, core = position()
    for n, out in enumerate(outs):
        k = start + n
        first = (target(c, k) * 2 + core) * pieces
        for p in range(pieces):
            rows = slice(p * tile, (p + 1) * tile)
            out[rows, :] = (acc[first + p] + other[n, rows, :].astype(F32)).astype(BF16)


def back_kernel(jobs, values, panel, w, x1, x2, x3, y1, x0, y0, vals, gs, acc, sem):
    s, _, _ = position()
    per, tile = values.shape[0] // N, values.shape[1]
    pieces = gs.shape[1] // tile
    half = pieces // 2
    copies = [pltpu.make_async_copy(panel, gs, sem.at[N])]
    for k in ORDER:
        rows = pl.ds(target(s, k) * per, per)
        copies.append(pltpu.make_async_copy(values.at[rows], vals.at[rows], sem.at[k]))
    for copy in copies:
        copy.start()
    acc[...] = jnp.zeros_like(acc)
    vals[N * per] = jnp.zeros(vals.shape[1:], vals.dtype)
    xs = (x0, x1, x2, x3)
    for out in xs[1:]:
        out[2 * half * tile :, :] = w[...].astype(BF16)
    for high in range(2):
        for copy in copies[5:] if high else copies[:5]:
            copy.wait()
        base = high * (4 * pieces + 1)

        def rows_of(g):
            return gs[g // pieces, pl.ds(pl.multiple_of((g % pieces) * tile, tile), tile), :]

        def body(q, ta, ga, tb, gb):
            both = jnp.concatenate([vals[ta], vals[tb]], axis=0)
            blocks = jnp.concatenate([rows_of(ga), rows_of(gb)], axis=0)
            acc[base + q] += lax.dot_general(both, blocks, (((0,), (0,)), ((), ())), preferred_element_type=F32)

        run_pairs(high, jobs, body)
        y = (y0, y1)[high]
        for b in range(4):
            for p in range(half):
                out, row = xs[b], (high * half + p) * tile
                out[row : row + tile, :] = acc[base + b * pieces + p].astype(out.dtype)
                row = (b * half + p) * tile
                y[row : row + tile, :] = acc[base + b * pieces + half + p].astype(y.dtype)


def middle_kernel(w, x0, y0, y1, x1, x3, x2, message, z1, z2, z3, top, low):
    rows = top.shape[0]
    message[rows : rows + w.shape[0], :] = w[...].astype(BF16)
    for b, x in enumerate((x1, x2, x3), 1):
        at = rows + b * w.shape[0]
        message[at : at + w.shape[0], :] = x[2 * rows :, :]
    sums = x0[...]
    for x in (x1, x2, x3):
        sums = sums + x[: 2 * rows, :].astype(F32)
    top[...] = sums[:rows, :]
    message[:rows, :] = sums[rows:, :].astype(BF16)
    for b, z in enumerate((low, z1, z2, z3)):
        at = slice(b * rows, (b + 1) * rows)
        z[...] = (y0[at, :] + y1[at, :].astype(F32)).astype(z.dtype)


def dense_kernel(*refs):
    parts, (cot, weight), (act, agg_grad, term) = refs[:N], refs[N : N + 2], refs[N + 2 :]
    agg = parts[0][...].astype(F32)
    for part in parts[1:]:
        agg = agg + part[...].astype(F32)
    low = agg.astype(BF16)
    pre = jnp.dot(low, weight[...], preferred_element_type=F32)
    root = 0.7978845608028654
    square = pre * pre
    t = jnp.tanh(root * pre * (1.0 + 0.044715 * square))
    act[...] = (0.5 * pre * (1.0 + t)).astype(BF16)
    slope = 0.5 * (1.0 + t) + 0.5 * pre * (1.0 - t * t) * (root * (1.0 + 3.0 * 0.044715 * square))
    pre_grad = (cot[...].astype(F32) * slope).astype(BF16)
    term[...] = lax.dot_general(low, pre_grad, (((0,), (0,)), ((), ())), preferred_element_type=F32)
    agg_grad[...] = lax.dot_general(
        pre_grad, weight[...], (((1,), (1,)), ((), ())), preferred_element_type=F32
    ).astype(BF16)


def finish_kernel(order, own, got, top, low, z1, z2, z3, out, grad):
    s, _, _ = position()
    rows = top.shape[0]
    part = grad.shape[0] // N
    for high, message in enumerate((own, got)):
        for b in range(4):
            at = pl.multiple_of(source(s, high * 4 + b) * part, part)
            grad[pl.ds(at, part), :] = message[rows + b * part : rows + (b + 1) * part, :].astype(F32)
    upper = (top[...] + got[:rows, :].astype(F32)).astype(BF16)
    lower = low[...]
    for z in (z1, z2, z3):
        lower = lower + z[...].astype(F32)
    total = jnp.concatenate([upper, lower.astype(BF16)], axis=0)
    blk = total.shape[0]
    place = lax.broadcasted_iota(jnp.int32, (blk, blk), 0) == order[...]
    out[...] = jnp.dot(place.astype(BF16), total, preferred_element_type=F32).astype(BF16)


def reorder_kernel(order, features, out):
    blk = features.shape[0]
    pick = lax.broadcasted_iota(jnp.int32, (blk, blk), 0) == order[...]
    out[...] = lax.dot_general(
        pick.astype(BF16), features[...], (((0,), (0,)), ((), ())), preferred_element_type=F32
    ).astype(BF16)


VMEM = pl.BlockSpec(memory_space=pltpu.VMEM)
SMEM = pl.BlockSpec(memory_space=pltpu.SMEM)
HBM = pl.BlockSpec(memory_space=pltpu.HBM)
MIB = 1 << 20


def shards(features, order, tile_rows, tile_cols, tile_live, tile_values, weight, cotangent):
    blk, width = features.shape
    tile = tile_values.shape[-1]
    pieces = blk // tile
    half = blk // 2
    values = tile_values[0, 0]
    s = lax.axis_index("section")
    d = lax.axis_index("dom")
    c, core = d >> 1, d & 1
    block = jax.ShapeDtypeStruct((blk, width), BF16)
    held = pltpu.VMEM((blk, width), BF16)
    stack = pltpu.VMEM((2 * N * pieces + 1, tile, width), F32)
    params = pltpu.CompilerParams(vmem_limit_bytes=24 * MIB)

    def together(*arrays):
        return lax.optimization_barrier(arrays)

    reordered = pl.pallas_call(
        reorder_kernel, out_shape=held, in_specs=[VMEM] * 2, out_specs=VMEM, name="reorder"
    )(order, features)
    first = {k: to_section(reordered, k) if k else reordered for k in NEAR}
    tiles = (tile_live[0, 0] << 16) | (tile_rows[0, 0] << 8) | tile_cols[0, 0]
    stored = values
    values, acc, jobs, own = pl.pallas_call(
        prepare_kernel,
        out_shape=[
            pltpu.VMEM(stored.shape, BF16),
            stack,
            jax.ShapeDtypeStruct((2 * LIST + 2,), jnp.int32),
            held,
        ],
        in_specs=[SMEM, HBM, VMEM],
        out_specs=[VMEM] * 2 + [SMEM, VMEM],
        scratch_shapes=[pltpu.SemaphoreType.DMA((2,))],
        compiler_params=pltpu.CompilerParams(vmem_limit_bytes=44 * MIB),
        name="prepare",
    )(tiles, stored, reordered)
    first[2], first[4], acc = together(first[2], first[4], acc)
    second = {5: to_section(first[4], 1), 7: to_section(first[4], 3), 6: to_section(first[2], 4)}
    flops = 96 * tile * tile * width * 2
    cost = pl.CostEstimate(flops=flops, bytes_accessed=12 * MIB, transcendentals=0)
    acc = pl.pallas_call(
        near_kernel,
        out_shape=stack,
        in_specs=[SMEM] + [VMEM] * (len(NEAR) + 2),
        out_specs=VMEM,
        scratch_shapes=[pltpu.VMEM((len(NEAR), blk, width), BF16), pltpu.SemaphoreType.DMA((len(NEAR),))],
        input_output_aliases={2: 0},
        compiler_params=params,
        cost_estimate=cost,
        name="aggregate_near",
    )(jobs, values, acc, *[first[k] if k else own for k in NEAR])
    four = pltpu.VMEM((N // 2, blk, width), BF16)
    acc, across, along = pl.pallas_call(
        far_kernel,
        out_shape=[stack, four, four],
        in_specs=[SMEM] + [VMEM] * (len(FAR) + 2),
        out_specs=[VMEM] * 3,
        scratch_shapes=[pltpu.VMEM((len(FAR), blk, width), BF16), pltpu.SemaphoreType.DMA((len(FAR),))],
        input_output_aliases={2: 0},
        compiler_params=params,
        cost_estimate=cost,
        name="aggregate_far",
    )(jobs, values, acc, *[second[k] for k in FAR])

    def pair_sums(start, other):
        return pl.pallas_call(
            functools.partial(pair_kernel, start),
            out_shape=[held] * (N // 2),
            in_specs=[VMEM] * 2,
            out_specs=[VMEM] * (N // 2),
            compiler_params=params,
            name=f"pair_{start}",
        )(acc, other)

    across, along = to_core(across), to_core(along)
    far_sums = pair_sums(N // 2, across)
    near_sums = pair_sums(0, along)
    sums = [*near_sums, *far_sums]
    back_jobs = pl.pallas_call(
        functools.partial(prepare_back_kernel, pieces),
        out_shape=jax.ShapeDtypeStruct((2 * LIST + 2,), jnp.int32),
        in_specs=[SMEM, VMEM],
        out_specs=SMEM,
        scratch_shapes=[pltpu.SMEM((stored.shape[0] * pieces,), jnp.int32), pltpu.SMEM((N * pieces,), jnp.int32)],
        name="prepare_back",
    )(tiles, sums[0])
    sums[1], jobs = together(sums[1], back_jobs)
    arrived = [to_chip(sums[k], k) if k else sums[k] for k in (1, 3, 6, 5, 7, 4, 2, 0)]

    activated, agg_grad, term = pl.pallas_call(
        dense_kernel,
        out_shape=[block, block, pltpu.VMEM((width, width), F32)],
        in_specs=[VMEM] * (N + 2),
        out_specs=[VMEM] * 3,
        compiler_params=params,
        name="dense",
    )(*arrived, cotangent, weight)

    def swap(x, axis, bit):
        n = lax.axis_size(axis)
        return lax.ppermute(x, axis, [(i, i ^ bit) for i in range(n)])

    def halve(x, bit):
        n = x.shape[0] // 2
        high = (s & bit) != 0
        keep = jnp.where(high, x[n:], x[:n])
        return keep + swap(jnp.where(high, x[:n], x[n:]), "section", bit)

    panel = lax.all_gather(agg_grad, "dom", axis=0)
    w = halve(halve(term, 4), 2)
    w = halve(w, 1)
    for bit in (8, 4, 2, 1):
        w = w + swap(w, "dom", bit)
    panel, w = together(panel, w)
    part = w.shape[0]

    def wide(rows, dtype=BF16):
        return pltpu.VMEM((rows, width), dtype)

    x1, x2, x3, y1, x0, y0 = pl.pallas_call(
        back_kernel,
        out_shape=[wide(blk + part)] * 3 + [wide(2 * blk), wide(blk, F32), wide(2 * blk, F32)],
        in_specs=[SMEM] + [HBM] * 2 + [VMEM],
        out_specs=[VMEM] * 6,
        scratch_shapes=[
            pltpu.VMEM((stored.shape[0] + 1, tile, tile), BF16),
            pltpu.VMEM(panel.shape, BF16),
            pltpu.VMEM((N * pieces + 2, tile, width), F32),
            pltpu.SemaphoreType.DMA((N + 1,)),
        ],
        compiler_params=pltpu.CompilerParams(vmem_limit_bytes=56 * MIB),
        cost_estimate=cost,
        name="aggregate_back",
    )(jobs, stored, panel, w)
    message, z1, z2, z3, top, low = pl.pallas_call(
        middle_kernel,
        out_shape=[wide(half + 4 * part)] + [wide(half)] * 3 + [wide(half, F32)] * 2,
        in_specs=[VMEM] * 7,
        out_specs=[VMEM] * 6,
        compiler_params=params,
        name="middle",
    )(w, x0, y0, to_section(y1, 4), to_section(x1, 1), to_section(x3, 3), to_section(x2, 2))
    feature_grad, weight_grad = pl.pallas_call(
        finish_kernel,
        out_shape=[block, jax.ShapeDtypeStruct((width, width), F32)],
        in_specs=[VMEM] * 8,
        out_specs=[VMEM] * 2,
        compiler_params=params,
        name="finish",
    )(
        order, message, to_section(message, 4), top, low, to_section(z1, 1), to_section(z2, 2), to_section(z3, 3)
    )
    return (activated, feature_grad, weight_grad)


def solution(mesh):
    return jax.shard_map(
        shards,
        mesh=mesh,
        in_specs=(
            P(("section", "dom"), None),
            P(("section", "dom"), None),
            P("section", "dom", None),
            P("section", "dom", None),
            P("section", "dom", None),
            P("section", "dom", None, None, None),
            P(),
            P(("section", "dom"), None),
        ),
        out_specs=(P(("section", "dom"), None), P(("section", "dom"), None), P()),
        check_vma=False,
    )
```
